32 devices in a mesh: fsdp: 8 (over z, x), ctx: 2 (over core), tp: 2 (over y).
Axes of the slice: x: 2, y: 2, z: 4, core: 2. Of those that a mesh axis runs over, the one named last changes fastest.
Arguments:
- inputs: bfloat16 [8, 320, 1024], P('fsdp', 'ctx'), may hold values from -11 to 11, as said below
- lengths: int32 [8], P('fsdp'), may hold values from 224 to 320, as said below
- grad_out: bfloat16 [8, 320, 1024], P('fsdp', 'ctx'), may hold values from -6 to 6
- ln1_gain: bfloat16 [1024], P(('fsdp', 'ctx')), may hold values from 0.099609375 to 1.8984375
- ln1_shift: bfloat16 [1024], P(('fsdp', 'ctx')), may hold values from -3 to 3
- w_qkv: bfloat16 [1024, 3, 1024], P(('fsdp', 'ctx'), None, 'tp'), may hold values from -0.1875 to 0.1875
- b_qv: bfloat16 [1024, 2], P(('fsdp', 'ctx'), 'tp'), may hold values from -3 to 3
- w_proj: bfloat16 [1024, 1024], P(('fsdp', 'ctx'), 'tp'), may hold values from -0.5 to 0.5
- b_proj: bfloat16 [1024], P(('fsdp', 'ctx')), may hold values from -3 to 3
- ln2_gain: bfloat16 [1024], P(('fsdp', 'ctx')), may hold values from 0.099609375 to 1.8984375
- ln2_shift: bfloat16 [1024], P(('fsdp', 'ctx')), may hold values from -3 to 3
- w_up: bfloat16 [1024, 4096], P(('fsdp', 'ctx'), 'tp'), may hold values from -0.1875 to 0.1875
- b_up: bfloat16 [2048, 2], P(('fsdp', 'ctx'), 'tp'), may hold values from -3 to 3
- w_down: bfloat16 [1024, 4096], P(('fsdp', 'ctx'), 'tp'), may hold values from -0.09375 to 0.09375
- b_down: bfloat16 [1024], P(('fsdp', 'ctx')), may hold values from -3 to 3
Outputs:
- output: bfloat16 [8, 320, 1024], P('fsdp', 'ctx')
- grad_inputs: float32 [8, 320, 1024], P('fsdp', 'ctx')
- grad_ln1_gain: float32 [1024], P(('fsdp', 'ctx'))
- grad_ln1_shift: float32 [1024], P(('fsdp', 'ctx'))
- grad_w_qkv: float32 [1024, 3, 1024], P(('fsdp', 'ctx'), None, 'tp')
- grad_b_qv: float32 [1024, 2], P(('fsdp', 'ctx'), 'tp')
- grad_w_proj: float32 [1024, 1024], P(('fsdp', 'ctx'), 'tp')
- grad_b_proj: float32 [1024], P(('fsdp', 'ctx'))
- grad_ln2_gain: float32 [1024], P(('fsdp', 'ctx'))
- grad_ln2_shift: float32 [1024], P(('fsdp', 'ctx'))
- grad_w_up: float32 [1024, 4096], P(('fsdp', 'ctx'), 'tp')
- grad_b_up: float32 [2048, 2], P(('fsdp', 'ctx'), 'tp')
- grad_w_down: float32 [1024, 4096], P(('fsdp', 'ctx'), 'tp')
- grad_b_down: float32 [1024], P(('fsdp', 'ctx'))
- rms: float32 [5], replicated
The draws below stay inside these ranges and needn't reach their ends.
Inputs may be any that keep to these rules, and one draw needn't show every extreme that they name: The lengths 320 and 224 both occur in every draw. `inputs`: rows at or past an image's length are never read.
All inputs are finite; a program needn't handle non-finite values.
Results may differ from the reference program's by a relative error of at most 0.014.
Values may be sent and summed in bfloat16 or wider, within the bound.
No kernel may reach another device: no remote copies, remote signals or barrier semaphores. Data moves between devices by JAX's collectives and lax.ppermute only.
A program may use at most 128 MiB of HBM per device.

```python
import math
import jax
import jax.numpy as jnp
from jax import lax

D = 1024
H = 16
HD = 64
FF = 4096
SLOTS = 320
MIN_LEN = 224
N_IMG = 8
N_TP = 2


def draw_lengths(key, part):
    drawn = jax.random.randint(jax.random.fold_in(key, 7), (N_IMG,), MIN_LEN, SLOTS + 1)
    image_ids = jnp.arange(N_IMG, dtype=jnp.int32)
    drawn = jnp.where(image_ids == 0, SLOTS, drawn)
    drawn = jnp.where(image_ids == 1, MIN_LEN, drawn)
    return drawn.astype(jnp.int32)


def draw_inputs(key, part):
    first_key = jax.random.fold_in(key, 3)
    second_key = jax.random.fold_in(key, 5)
    position = jnp.arange(N_IMG, dtype=jnp.float32) / (N_IMG - 1)
    base_values = jnp.clip(jax.random.normal(first_key, (N_IMG, SLOTS, D), jnp.float32), -4.0, 4.0)
    row_scale = 0.9 + 0.2 * jax.random.uniform(second_key, (N_IMG, SLOTS, 1), jnp.float32)
    ramp = 0.5 + position
    return (base_values * row_scale * ramp[:, None, None]).astype(jnp.bfloat16)


def with_spikes(array, rng, source, target, blocks, factor):
    def block_of(axis_at):
        return (jnp.arange(array.shape[axis_at]) // (array.shape[axis_at] // blocks)).reshape((-1,) + (1,) * (array.ndim - 1 - axis_at))

    near = jax.random.permutation(rng, blocks)[block_of(target)]
    far = (block_of(target) + blocks // 2) % blocks
    return jnp.where((block_of(source) == near) | (block_of(source) == far), factor * array, array)


def level_of(stream_key, shape, cuts, least, high):
    level = 1.0
    for dim, parts in cuts:
        heights = jax.random.uniform(jax.random.fold_in(jax.random.fold_in(stream_key, 6), dim), (parts,), jnp.float32, least / len(cuts), high / len(cuts))
        level = level * jnp.repeat(jnp.exp(heights), shape[dim] // parts).reshape((-1,) + (1,) * (len(shape) - 1 - dim))
    return level


def normal_values(own_key, extent, width, bound, split=(), held_as=jnp.bfloat16):
    factor_of = level_of(own_key, extent, split, -0.22, 0.18) if split else 1.0
    array = jax.random.normal(own_key, extent, jnp.float32) * width * factor_of
    return jnp.minimum(jnp.maximum(array, -bound), bound).astype(held_as)


def noise_with(rng, extent, deviation, reach, cuts, heavy, held_as=jnp.bfloat16):
    values = deviation * jax.random.normal(rng, extent, jnp.float32)
    if cuts:
        values = values * level_of(rng, extent, cuts, -0.22, 0.18)
    return jnp.clip(with_spikes(values, jax.random.fold_in(rng, 3), *heavy), -reach, reach).astype(held_as)


def setup_inputs(seed: int = 0) -> dict:
    streams_of = jax.random.split(jax.random.key(seed), 16)
    return {
        "inputs": draw_inputs(jax.random.fold_in(streams_of[15], 71), 0),
        "lengths": draw_lengths(jax.random.fold_in(streams_of[15], 71), 0),
        "grad_out": noise_with(streams_of[2], (N_IMG, SLOTS, D), 1.0, 6.0, ((0, 8), (1, 2)), (0, 2, 8, 2.0)),
        "ln1_gain": jnp.clip(1.0 + 0.18 * jax.random.normal(streams_of[3], (D,), jnp.float32), 0.099609375, 1.8984375).astype(jnp.bfloat16),
        "ln1_shift": normal_values(streams_of[4], (D,), 0.5, 3.0, ((0, 16),)),
        "w_qkv": normal_values(streams_of[5], (D, 3, D), D ** -0.5, 0.1875, ((0, 16), (2, 2))),
        "b_qv": normal_values(streams_of[6], (2 * D // N_TP, N_TP), 0.5, 3.0, ((0, 16), (1, 2))),
        "w_proj": normal_values(streams_of[7], (D, D), (D // 8) ** -0.5, 0.5, ((0, 16), (1, 2))),
        "b_proj": normal_values(streams_of[8], (D,), 0.5, 3.0, ((0, 16),)),
        "ln2_gain": jnp.clip(1.0 + 0.18 * jax.random.normal(streams_of[9], (D,), jnp.float32), 0.099609375, 1.8984375).astype(jnp.bfloat16),
        "ln2_shift": normal_values(streams_of[10], (D,), 0.5, 3.0, ((0, 16),)),
        "w_up": normal_values(streams_of[11], (D, FF), D ** -0.5, 0.1875, ((0, 16), (1, 2))),
        "b_up": normal_values(streams_of[12], (FF // N_TP, N_TP), 0.5, 3.0, ((0, 16), (1, 2))),
        "w_down": normal_values(streams_of[13], (D, FF), FF ** -0.5, 0.09375, ((0, 16), (1, 2))),
        "b_down": normal_values(streams_of[14], (D,), 0.5, 3.0, ((0, 16),)),
    }


EPSILON = 1e-06
MASK_FILL = -1e+30
PRECISE = lax.Precision.HIGHEST

@jax.custom_vjp
def low(v):
    return lax.optimization_barrier(v.astype(jnp.bfloat16)).astype(jnp.float32)

@jax.custom_vjp
def low_back(v):
    return v

def low_keep(v):
    return (low(v), None)

def low_pass(kept, grad):
    return (grad,)

def back_keep(v):
    return (v, None)

def back_low(kept, grad):
    return (low(grad),)
low.defvjp(low_keep, low_pass)
low_back.defvjp(back_keep, back_low)

def layer_norm(values_in, gain, shift):
    mean_val = lax.optimization_barrier(jnp.mean(values_in, axis=-1, keepdims=True))
    centered = values_in - mean_val
    spread = lax.optimization_barrier(jnp.mean(centered * centered, axis=-1, keepdims=True))
    return centered * lax.rsqrt(spread + EPSILON) * gain + shift

def layer(inputs_in, is_valid, weights):
    gain_one, shift_one, w_qkv, b_qv, w_proj, b_proj, gain_two, shift_two, w_up, b_up, w_down, b_down = weights
    images, slot_count = is_valid.shape
    entering = inputs_in * is_valid[:, :, None]
    normed = low(layer_norm(entering, gain_one, shift_one))
    packed = jnp.einsum('bsd,dce->bsce', normed, w_qkv, precision=PRECISE)
    query_bias = b_qv[:D // N_TP].T.reshape(D)
    value_bias = b_qv[D // N_TP:].T.reshape(D)
    head_shape = (images, slot_count, H, HD)
    query_part = low(low_back(packed[:, :, 0] + query_bias)).reshape(head_shape)
    key_part = low(low_back(packed[:, :, 1])).reshape(head_shape)
    value_part = low(low_back(packed[:, :, 2] + value_bias)).reshape(head_shape)
    scores = low_back(jnp.einsum('bqhd,bkhd->bhqk', query_part, key_part, precision=PRECISE) * HD ** (-0.5))
    key_mask = is_valid[:, None, None, :] > 0
    scores = jnp.where(key_mask, scores, MASK_FILL)
    row_max = lax.optimization_barrier(jnp.max(scores, axis=-1, keepdims=True))
    raised = jnp.exp(scores - row_max)
    attn_prob = raised / lax.optimization_barrier(jnp.sum(raised, axis=-1, keepdims=True))
    context = jnp.einsum('bhqk,bkhd->bqhd', low(attn_prob), value_part, precision=PRECISE)
    context = low(low_back(context.reshape(images, slot_count, D)))
    attended = low_back(jnp.einsum('bse,de->bsd', context, w_proj, precision=PRECISE) + b_proj)
    middle = entering + attended
    normed_two = low(layer_norm(middle, gain_two, shift_two))
    pre_act = low_back(jnp.einsum('bsd,df->bsf', normed_two, w_up, precision=PRECISE) + b_up.T.reshape(FF))
    active = low(jax.nn.gelu(pre_act, approximate=False))
    branch = low_back(jnp.einsum('bsf,df->bsd', active, w_down, precision=PRECISE) + b_down)
    result = middle + branch
    mask_rows = is_valid[:, :, None]
    squares = jnp.stack([jnp.sum(mask_rows * stat_term * stat_term) for stat_term in (entering, attended, middle, branch, result)])
    return (result, squares)

def reference(inputs, lengths, grad_out, ln1_gain, ln1_shift, w_qkv, b_qv, w_proj, b_proj, ln2_gain, ln2_shift, w_up, b_up, w_down, b_down):
    params = tuple((weight_arg.astype(jnp.float32) for weight_arg in (ln1_gain, ln1_shift, w_qkv, b_qv, w_proj, b_proj, ln2_gain, ln2_shift, w_up, b_up, w_down, b_down)))
    batch_images = math.gcd(inputs.shape[0], 8)
    groups = inputs.shape[0] // batch_images
    shaped = (groups, batch_images, SLOTS, D)
    slot_ids = jnp.arange(SLOTS, dtype=jnp.int32)

    def group_step(carry, pieces):
        grad_sums, stat_sums = carry
        block_in, block_len, block_grad = pieces
        is_valid = (slot_ids[None, :] < block_len[:, None].astype(jnp.int32)).astype(jnp.float32)

        def forward(inputs_in, weights):
            return layer(inputs_in, is_valid, weights)
        result, pullback, squares = jax.vjp(forward, block_in.astype(jnp.float32), params, has_aux=True)
        grad_in, grad_weights = pullback(block_grad.astype(jnp.float32))
        grad_sums = jax.tree.map(jnp.add, grad_sums, grad_weights)
        stat_sums = stat_sums + jnp.concatenate([squares, jnp.sum(is_valid)[None]])
        return ((grad_sums, stat_sums), (result.astype(jnp.bfloat16), grad_in))
    initial = (jax.tree.map(jnp.zeros_like, params), jnp.zeros((6,), jnp.float32))
    (grad_sums, stat_sums), (outputs, grad_inputs) = lax.scan(group_step, initial, (inputs.reshape(shaped), lengths.reshape(groups, batch_images), grad_out.reshape(shaped)))
    rms = jnp.sqrt(stat_sums[:5] / (stat_sums[5] * D))
    whole = (groups * batch_images, SLOTS, D)
    return (outputs.reshape(whole), grad_inputs.reshape(whole), grad_sums[0], grad_sums[1], grad_sums[2], grad_sums[3], grad_sums[4], grad_sums[5], grad_sums[6], grad_sums[7], grad_sums[8], grad_sums[9], grad_sums[10], grad_sums[11], rms)
```

```python
import jax
import jax.numpy as jnp
from jax import lax
from jax.sharding import PartitionSpec as P

D = 1024
HD = 64
EPSILON = 1e-06
MASK_FILL = -1e30
ROOT_HALF = 0.7071067811865476
INV_ROOT_TWO_PI = 0.3989422804014327
F32 = jnp.float32
BF16 = jnp.bfloat16
MAX_DEPTH = 4


def contract(left, right, left_dim, right_dim):
    return lax.dot_general(
        left, right, (((left_dim,), (right_dim,)), ((), ())), preferred_element_type=F32
    )


def round_low(values):
    return lax.reduce_precision(values, 8, 7).astype(BF16)


def swap(array, axis):
    return lax.ppermute(array, axis, [(0, 1), (1, 0)])


def swap_x(array):
    n = lax.axis_size("fsdp")
    return lax.ppermute(array, "fsdp", [(i, i ^ 1) for i in range(n)])


def shift_z(array, steps):
    n = lax.axis_size("fsdp")
    return lax.ppermute(array, "fsdp", [(i, (i + 2 * steps) % n) for i in range(n)])


def relative_blocks():
    depth = lax.axis_size("fsdp") // 2
    place = lax.axis_index("fsdp")
    spots = jnp.arange(2 * depth, dtype=jnp.int32)
    return ((spots % 2) ^ (place % 2)) * depth + (place // 2 - spots // 2) % depth


def absolute_places():
    depth = lax.axis_size("fsdp") // 2
    place = lax.axis_index("fsdp")
    blocks = jnp.arange(2 * depth, dtype=jnp.int32)
    return ((place // 2 - blocks % depth) % depth) * 2 + ((place % 2) ^ (blocks // depth))


def gather_pieces(shard):
    depth = lax.axis_size("fsdp") // 2
    if depth > MAX_DEPTH:
        gathered = jnp.take(lax.all_gather(shard, "fsdp"), absolute_places(), axis=0)
        return [gathered[i] for i in range(2 * depth)]
    near = [shard] + [shift_z(shard, k) for k in range(1, depth)]
    far = [swap_x(piece) for piece in near]
    return near + far


def scatter_sum(partial):
    depth = lax.axis_size("fsdp") // 2
    half = partial.shape[0] // 2
    block = half // depth
    if depth > MAX_DEPTH:
        blocks = round_low(partial).reshape(2 * depth, block, -1)
        blocks = jnp.take(blocks, relative_blocks(), axis=0).reshape(partial.shape)
        return lax.psum_scatter(blocks, "fsdp", scatter_dimension=0, tiled=True).astype(F32)
    arrived = swap_x(round_low(partial[half:]))
    both = partial[:half] + arrived.astype(F32)
    total = both[:block]
    for k in range(1, depth):
        total = total + shift_z(
            round_low(both[k * block : (k + 1) * block]), -k
        ).astype(F32)
    return total


def image_sum(partial):
    half = partial.shape[0] // 2
    own = partial[:half] + swap(round_low(partial[half:]), "ctx").astype(F32)
    low = round_low(own)
    return low.astype(F32) + swap(low, "tp").astype(F32)


def with_other(own):
    return jnp.concatenate([own, swap(own, "ctx")], axis=0)


def stats_of(values):
    mean = jnp.mean(values, axis=-1, keepdims=True)
    centered = values - mean
    scale = lax.rsqrt(jnp.mean(centered * centered, axis=-1, keepdims=True) + EPSILON)
    return centered * scale, scale


def norm_back(normal, scale, gain, grad):
    weighted = grad * gain
    grad_in = scale * (
        weighted
        - jnp.mean(weighted, axis=-1, keepdims=True)
        - normal * jnp.mean(weighted * normal, axis=-1, keepdims=True)
    )
    return grad_in, jnp.sum(grad * normal, axis=0), jnp.sum(grad, axis=0)


def body(
    inputs,
    lengths,
    grad_out,
    ln1_gain,
    ln1_shift,
    w_qkv,
    b_qv,
    w_proj,
    b_proj,
    ln2_gain,
    ln2_shift,
    w_up,
    b_up,
    w_down,
    b_down,
):
    n = lax.axis_size("fsdp")
    depth = n // 2
    core = lax.axis_index("ctx")
    place = lax.axis_index("fsdp")
    rows = w_up.shape[0]
    head_cols = w_proj.shape[1] // 2
    hidden = w_up.shape[1] // 2
    own_slots = inputs.shape[1]
    width = D // n

    qkv_halves = w_qkv.reshape(rows, 3, 2, head_cols)
    proj_halves = w_proj.reshape(rows, 2, head_cols)
    up_halves = w_up.reshape(rows, 2, hidden)
    down_halves = w_down.reshape(rows, 2, hidden)

    def half_of(which):
        first = jnp.concatenate(
            [
                lax.dynamic_index_in_dim(qkv_halves, which, 2, keepdims=False).reshape(
                    rows, 3 * head_cols
                ),
                lax.dynamic_index_in_dim(proj_halves, which, 1, keepdims=False),
            ],
            axis=1,
        )
        return (
            first,
            lax.dynamic_index_in_dim(up_halves, which, 1, keepdims=False),
            lax.dynamic_index_in_dim(down_halves, which, 1, keepdims=False),
        )

    def by_core(own, other, axis):
        return jnp.where(
            core == 0,
            jnp.concatenate([own, other], axis=axis),
            jnp.concatenate([other, own], axis=axis),
        )

    small = jnp.concatenate(
        [
            jnp.stack([ln1_gain, ln1_shift, b_proj, ln2_gain, ln2_shift, b_down, b_qv[:, 0]]),
            b_up.reshape(2, rows),
        ]
    )
    small_both = by_core(small, swap(small, "ctx"), 1)
    own_parts, other_parts = half_of(core), half_of(1 - core)
    shards = [by_core(own, swap(other, "ctx"), 0) for own, other in zip(own_parts, other_parts)]
    small_flat = jnp.zeros((16 * 2 * rows,), BF16)
    small_flat = small_flat.at[: 9 * 2 * rows].set(small_both.reshape(-1))
    cols = shards[0].shape[1]
    small_rows = -(-16 * 2 * rows // cols)
    small_rows_padded = -(-small_rows // 8) * 8
    small_block = jnp.zeros((small_rows_padded * cols,), BF16)
    small_block = small_block.at[: 16 * 2 * rows].set(small_flat).reshape(small_rows_padded, cols)

    first_pieces = gather_pieces(jnp.concatenate([shards[0], small_block], axis=0))
    up_pieces = gather_pieces(shards[1])
    down_pieces = gather_pieces(shards[2])
    first_full = jnp.concatenate([p[: 2 * rows] for p in first_pieces], axis=0)
    qkv_full = first_full[:, : 3 * head_cols]
    proj_full = first_full[:, 3 * head_cols :]
    up_full = jnp.concatenate(up_pieces, axis=0)
    down_full = jnp.concatenate(down_pieces, axis=0)
    small_all = jnp.stack([p[2 * rows :].reshape(-1)[: 16 * 2 * rows] for p in first_pieces])
    small_all = small_all.reshape(n, 16, 2 * rows)
    vectors = small_all.transpose(1, 0, 2).reshape(16, D).astype(F32)
    gain_one, shift_one, proj_bias, gain_two, shift_two, down_bias = (vectors[i] for i in range(6))
    absolute, relative = absolute_places(), relative_blocks()
    small_abs = jnp.take(small_all, relative, axis=0).astype(F32)
    qv_all = small_abs[:, 6].reshape(2, 2, head_cols)
    qv_bias = lax.dynamic_index_in_dim(qv_all, core, 1, keepdims=False)
    up_all = small_abs[:, 7:9].reshape(n, 2, 2, rows).transpose(0, 2, 1, 3).reshape(2, hidden)
    up_bias = lax.dynamic_index_in_dim(up_all, core, 0, keepdims=False)

    def to_relative(array):
        blocks = array.reshape(array.shape[0], n, width)
        return jnp.take(blocks, absolute, axis=1).reshape(array.shape)

    def to_absolute(array):
        blocks = array.reshape(array.shape[0], n, width)
        return jnp.take(blocks, relative, axis=1).reshape(array.shape)

    length = lengths[0]
    own_ids = core * own_slots + jnp.arange(own_slots, dtype=jnp.int32)
    other_ids = (1 - core) * own_slots + jnp.arange(own_slots, dtype=jnp.int32)
    slot_ids = jnp.concatenate([own_ids, other_ids])
    key_valid = slot_ids < length
    row_valid = key_valid.astype(F32)[:, None]
    own_valid = row_valid[:own_slots]

    entering_all = with_other(to_relative(inputs[0])).astype(F32) * row_valid
    grad_low = with_other(to_relative(grad_out[0]))
    grad_res = grad_low[:own_slots].astype(F32)
    normal_one, scale_one = stats_of(entering_all)
    normed = (normal_one * gain_one + shift_one).astype(BF16)
    packed = jnp.dot(normed, qkv_full, preferred_element_type=F32)
    slots = 2 * own_slots
    heads = head_cols // HD
    head_shape = (slots, heads, HD)
    query = (packed[:, :head_cols] + qv_bias[0]).astype(BF16).reshape(head_shape)
    key = packed[:, head_cols : 2 * head_cols].astype(BF16).reshape(head_shape)
    value = (packed[:, 2 * head_cols :] + qv_bias[1]).astype(BF16).reshape(head_shape)
    score_scale = HD ** (-0.5)
    scores = jnp.einsum("qhd,khd->hqk", query, key, preferred_element_type=F32) * score_scale
    scores = jnp.where(key_valid[None, None, :], scores, MASK_FILL)
    raised = jnp.exp(scores - jnp.max(scores, axis=-1, keepdims=True))
    prob = raised / jnp.sum(raised, axis=-1, keepdims=True)
    prob_low = prob.astype(BF16)
    context = jnp.einsum("hqk,khd->qhd", prob_low, value, preferred_element_type=F32)
    context = context.astype(BF16).reshape(slots, head_cols)
    attended = image_sum(contract(context, proj_full, 1, 1)) + proj_bias
    entering = entering_all[:own_slots]
    middle = entering + attended
    normal_two, scale_two = stats_of(middle)
    normed_two = with_other((normal_two * gain_two + shift_two).astype(BF16))
    pre_act = jnp.dot(normed_two, up_full, preferred_element_type=F32) + up_bias
    cumulative = 0.5 * (1.0 + lax.erf(pre_act * ROOT_HALF))
    active = (pre_act * cumulative).astype(BF16)
    slope = cumulative + pre_act * (INV_ROOT_TWO_PI * jnp.exp(-0.5 * pre_act * pre_act))
    branch = image_sum(contract(active, down_full, 1, 1)) + down_bias
    result = middle + branch
    output = to_absolute(result.astype(BF16))[None]
    square_sums = jnp.stack(
        [jnp.sum(own_valid * t * t) for t in (entering, attended, middle, branch, result)]
        + [jnp.sum(own_valid)]
    )

    sum_down_bias = jnp.sum(grad_res, axis=0)
    sum_down = scatter_sum(contract(grad_low, active, 0, 0))
    grad_active = jnp.dot(grad_low, down_full, preferred_element_type=F32)
    grad_pre = (grad_active * slope).astype(BF16)
    sum_up_bias = jnp.sum(grad_pre.astype(F32), axis=0)
    sum_up = scatter_sum(contract(normed_two, grad_pre, 0, 0))
    grad_normed_two = image_sum(contract(grad_pre, up_full, 1, 1))
    grad_mid_part, sum_gain_two, sum_shift_two = norm_back(
        normal_two, scale_two, gain_two, grad_normed_two
    )
    grad_middle = grad_res + grad_mid_part
    grad_att_own = grad_middle.astype(BF16)
    sum_proj_bias = jnp.sum(grad_att_own.astype(F32), axis=0)
    grad_att = with_other(grad_att_own)
    grad_proj = contract(grad_att, context, 0, 0)
    grad_context = (
        jnp.dot(grad_att, proj_full, preferred_element_type=F32).astype(BF16).reshape(head_shape)
    )
    grad_prob = jnp.einsum("qhd,khd->hqk", grad_context, value, preferred_element_type=F32)
    grad_scores = (
        prob * (grad_prob - jnp.sum(prob * grad_prob, axis=-1, keepdims=True))
    ).astype(BF16)
    grad_query = jnp.einsum("hqk,khd->qhd", grad_scores, key, preferred_element_type=F32)
    grad_key = jnp.einsum("hqk,qhd->khd", grad_scores, query, preferred_element_type=F32)
    grad_value = jnp.einsum("hqk,qhd->khd", prob_low, grad_context, preferred_element_type=F32)
    grad_query = (grad_query * score_scale).astype(BF16).reshape(slots, head_cols)
    grad_key = (grad_key * score_scale).astype(BF16).reshape(slots, head_cols)
    grad_value = grad_value.astype(BF16).reshape(slots, head_cols)
    sum_qv_bias = jnp.concatenate(
        [jnp.sum(grad_query.astype(F32), axis=0), jnp.sum(grad_value.astype(F32), axis=0)]
    )
    grad_packed = jnp.concatenate([grad_query, grad_key, grad_value], axis=1)
    sum_first = scatter_sum(
        jnp.concatenate([contract(normed, grad_packed, 0, 0), grad_proj], axis=1)
    )
    grad_normed = image_sum(contract(grad_packed, qkv_full, 1, 1))
    grad_enter, sum_gain_one, sum_shift_one = norm_back(
        normal_one[:own_slots], scale_one[:own_slots], gain_one, grad_normed
    )
    grad_inputs = to_absolute((grad_middle + grad_enter) * own_valid)[None]

    tail = jnp.concatenate(
        [sum_qv_bias, square_sums, jnp.zeros((D - 2 * head_cols - 6,), F32)]
    )
    per_core = jnp.stack(
        [
            sum_gain_one,
            sum_shift_one,
            sum_proj_bias,
            sum_gain_two,
            sum_shift_two,
            sum_down_bias,
            sum_up_bias.reshape(-1)[:D],
            tail,
        ]
    )
    if depth > MAX_DEPTH:
        vectors_sum = jnp.take(per_core[:6].reshape(6, n, width), relative, axis=1)
        vectors_sum = lax.psum(vectors_sum.reshape(6, D), "fsdp")
        vector_sum = lax.dynamic_slice_in_dim(vectors_sum, place * width, width, 1)
        rest_sum = lax.psum(per_core[6:], "fsdp")
    else:
        arrived = swap_x(per_core)
        turned = jnp.concatenate([arrived[:6, D // 2 :], arrived[:6, : D // 2]], axis=1)
        both = per_core + jnp.concatenate([turned, arrived[6:]], axis=0)
        vector_sum = both[:6, :width]
        rest_sum = both[6:]
        for k in range(1, depth):
            moved = shift_z(both, -k)
            vector_sum = vector_sum + moved[:6, k * width : (k + 1) * width]
            rest_sum = rest_sum + moved[6:]
    closing = jnp.zeros((8, D), F32).at[:6, :width].set(vector_sum).at[6:].set(rest_sum)
    other_closing = swap(closing, "ctx")
    vector_sum = vector_sum + other_closing[:6, :width]
    vector_own = lax.dynamic_slice_in_dim(vector_sum, core * rows, rows, 1)
    totals = (rest_sum[1] + other_closing[7])[2 * head_cols : 2 * head_cols + 6]
    rms = jnp.sqrt(totals[:5] / (totals[5] * D))
    qv_sum = by_core(
        rest_sum[1, : 2 * head_cols].reshape(2, 1, head_cols),
        other_closing[7, : 2 * head_cols].reshape(2, 1, head_cols),
        1,
    ).reshape(-1)
    qv_own = lax.dynamic_slice_in_dim(qv_sum, (2 * place + core) * rows, rows, 0)
    up_sum = by_core(rest_sum[0], other_closing[6], 0)
    up_own = lax.dynamic_slice_in_dim(up_sum, (2 * place + core) * 2 * rows, 2 * rows, 0)

    def owned(total):
        mine = lax.dynamic_slice_in_dim(total, core * rows, rows, 0)
        theirs = swap(lax.dynamic_slice_in_dim(total, (1 - core) * rows, rows, 0), "ctx")
        return mine, theirs

    mine, theirs = owned(sum_first)
    first_out = by_core(mine.reshape(rows, 4, 1, head_cols), theirs.reshape(rows, 4, 1, head_cols), 2)
    first_out = first_out.reshape(rows, 4, 2 * head_cols)
    grad_w_up = by_core(*owned(sum_up), 1)
    grad_w_down = by_core(*owned(sum_down), 1)
    return (
        output,
        grad_inputs,
        vector_own[0],
        vector_own[1],
        first_out[:, :3],
        qv_own[:, None],
        first_out[:, 3],
        vector_own[2],
        vector_own[3],
        vector_own[4],
        grad_w_up,
        up_own[:, None],
        grad_w_down,
        vector_own[5],
        rms,
    )


def solution(mesh):
    both = ("fsdp", "ctx")
    rows, vector, matrix = P("fsdp", "ctx", None), P(both), P(both, "tp")
    in_specs = (
        rows,
        P("fsdp"),
        rows,
        vector,
        vector,
        P(both, None, "tp"),
        matrix,
        matrix,
        vector,
        vector,
        vector,
        matrix,
        matrix,
        matrix,
        vector,
    )
    out_specs = (
        rows,
        rows,
        vector,
        vector,
        P(both, None, "tp"),
        matrix,
        matrix,
        vector,
        vector,
        vector,
        matrix,
        matrix,
        matrix,
        vector,
        P(),
    )
    return jax.shard_map(body, mesh=mesh, in_specs=in_specs, out_specs=out_specs, check_vma=False)
```

```python
import jax
import jax.numpy as jnp
from jax import lax
from jax.sharding import PartitionSpec as P

D = 1024
HD = 64
EPSILON = 1e-06
MASK_FILL = -1e30
ROOT_HALF = 0.7071067811865476
INV_ROOT_TWO_PI = 0.3989422804014327
F32 = jnp.float32
BF16 = jnp.bfloat16


def contract(left, right, left_dim, right_dim):
    return lax.dot_general(
        left, right, (((left_dim,), (right_dim,)), ((), ())), preferred_element_type=F32
    )


def round_low(values):
    return lax.reduce_precision(values, 8, 7).astype(BF16)


def swap(array, axis):
    return lax.ppermute(array, axis, [(0, 1), (1, 0)])


def flip(array, bit):
    n = lax.axis_size("fsdp")
    return lax.ppermute(array, "fsdp", [(i, i ^ bit) for i in range(n)])


X_BIT, NEAR_BIT, FAR_BIT = 1, 2, 4


def is_cube():
    return lax.axis_size("fsdp") == 8


def turned_bits(blocks):
    return (blocks % 2) * 4 + (blocks // 2 % 2) * 2 + blocks // 4


def relative_blocks():
    spots = jnp.arange(lax.axis_size("fsdp"), dtype=jnp.int32)
    if not is_cube():
        return spots
    return turned_bits(spots ^ lax.axis_index("fsdp"))


def absolute_places():
    blocks = jnp.arange(lax.axis_size("fsdp"), dtype=jnp.int32)
    if not is_cube():
        return blocks
    return turned_bits(blocks) ^ lax.axis_index("fsdp")


def tie(*values):
    return lax.optimization_barrier(values)


def rows_of(*pieces):
    return jnp.concatenate(pieces, axis=0)


def sent_half(left, right):
    return round_low(contract(left[:, left.shape[1] // 2 :], right, 0, 0))


def kept_half(left, right, arrived):
    return contract(left[:, : left.shape[1] // 2], right, 0, 0) + arrived.astype(F32)


def upper(array):
    return array[array.shape[0] // 2 :]


def lower(array):
    return array[: array.shape[0] // 2]


def scatter_sum(partial):
    low = round_low(partial)
    return lax.psum_scatter(low, "fsdp", scatter_dimension=0, tiled=True).astype(F32)


def image_sum(partial):
    half = partial.shape[0] // 2
    own = partial[:half] + swap(round_low(partial[half:]), "ctx").astype(F32)
    low = round_low(own)
    return low.astype(F32) + swap(low, "tp").astype(F32)


def with_other(own):
    return jnp.concatenate([own, swap(own, "ctx")], axis=0)


def stats_of(values):
    mean = jnp.mean(values, axis=-1, keepdims=True)
    centered = values - mean
    scale = lax.rsqrt(jnp.mean(centered * centered, axis=-1, keepdims=True) + EPSILON)
    return centered * scale, scale


def norm_back(normal, scale, gain, grad):
    weighted = grad * gain
    grad_in = scale * (
        weighted
        - jnp.mean(weighted, axis=-1, keepdims=True)
        - normal * jnp.mean(weighted * normal, axis=-1, keepdims=True)
    )
    return grad_in, jnp.sum(grad * normal, axis=0), jnp.sum(grad, axis=0)


def body(
    inputs,
    lengths,
    grad_out,
    ln1_gain,
    ln1_shift,
    w_qkv,
    b_qv,
    w_proj,
    b_proj,
    ln2_gain,
    ln2_shift,
    w_up,
    b_up,
    w_down,
    b_down,
):
    n = lax.axis_size("fsdp")
    cube = is_cube()
    core = lax.axis_index("ctx")
    place = lax.axis_index("fsdp")
    rows = w_up.shape[0]
    head_cols = w_proj.shape[1] // 2
    hidden = w_up.shape[1] // 2
    own_slots = inputs.shape[1]
    width = D // n

    qkv_halves = w_qkv.reshape(rows, 3, 2, head_cols)
    proj_halves = w_proj.reshape(rows, 2, head_cols)
    up_halves = w_up.reshape(rows, 2, hidden)
    down_halves = w_down.reshape(rows, 2, hidden)

    def first_half(which):
        return jnp.concatenate(
            [
                lax.dynamic_index_in_dim(qkv_halves, which, 2, keepdims=False).reshape(
                    rows, 3 * head_cols
                ),
                lax.dynamic_index_in_dim(proj_halves, which, 1, keepdims=False),
            ],
            axis=1,
        )

    def half_of(halves, which):
        return lax.dynamic_index_in_dim(halves, which, 1, keepdims=False)

    def by_core(own, other, axis):
        return jnp.where(
            core == 0,
            jnp.concatenate([own, other], axis=axis),
            jnp.concatenate([other, own], axis=axis),
        )

    small = jnp.concatenate(
        [
            jnp.stack([ln1_gain, ln1_shift, b_proj, ln2_gain, ln2_shift, b_down, b_qv[:, 0]]),
            b_up.reshape(2, rows),
        ]
    )
    small_both = by_core(small, swap(small, "ctx"), 1)
    first_own, first_other = first_half(core), first_half(1 - core)
    first_mine = by_core(first_own, swap(first_other, "ctx"), 0)
    small_flat = jnp.zeros((16 * 2 * rows,), BF16)
    small_flat = small_flat.at[: 9 * 2 * rows].set(small_both.reshape(-1))
    cols = first_mine.shape[1]
    small_rows = -(-16 * 2 * rows // cols)
    small_rows_padded = -(-small_rows // 8) * 8
    small_block = jnp.zeros((small_rows_padded * cols,), BF16)
    small_block = small_block.at[: 16 * 2 * rows].set(small_flat).reshape(small_rows_padded, cols)

    first_shard = jnp.concatenate([first_mine, small_block], axis=0)
    first_shard, inputs, grad_out, up_halves, down_halves = tie(
        first_shard, inputs, grad_out, up_halves, down_halves
    )
    u, d = (
        by_core(half_of(t, core), swap(half_of(t, 1 - core), "ctx"), 0)
        for t in (up_halves, down_halves)
    )
    f = first_shard
    if cube:
        f_far, f_x, u_x = flip(f, FAR_BIT), flip(f, X_BIT), flip(u, X_BIT)
        f_far, f_x, u_x, u, d = tie(f_far, f_x, u_x, u, d)
        f_near = flip(rows_of(f, f_far), NEAR_BIT)
        u_far, f_far_x, d_x = flip(u, FAR_BIT), flip(f_far, X_BIT), flip(d, X_BIT)
        f_near, u_far, f_far_x, d_x, u, d = tie(f_near, u_far, f_far_x, d_x, u, d)
        u_near = flip(rows_of(u, u_far), NEAR_BIT)
        d_far, f_near_x, u_far_x = flip(d, FAR_BIT), flip(f_near, X_BIT), flip(u_far, X_BIT)
        d_far, f_near_x, u_far_x, u_near, d = tie(d_far, f_near_x, u_far_x, u_near, d)
        d_near = flip(rows_of(d, d_far), NEAR_BIT)
        u_near_x, d_far_x = flip(u_near, X_BIT), flip(d_far, X_BIT)
        first_all = rows_of(f, f_far, f_near, f_x, f_far_x, f_near_x)
    else:
        first_all, up_full, down_full = (
            lax.all_gather(t, "fsdp", tiled=True) for t in (f, u, d)
        )
    first_all = first_all.reshape(n, 2 * rows + small_rows_padded, cols)
    first_full = first_all[:, : 2 * rows].reshape(D, cols)
    qkv_full = first_full[:, : 3 * head_cols]
    proj_full = first_full[:, 3 * head_cols :]
    small_all = first_all[:, 2 * rows :].reshape(n, -1)[:, : 16 * 2 * rows]
    small_all = small_all.reshape(n, 16, 2 * rows)
    vectors = small_all.transpose(1, 0, 2).reshape(16, D).astype(F32)
    gain_one, shift_one, proj_bias, gain_two, shift_two, down_bias = (vectors[i] for i in range(6))
    absolute, relative = absolute_places(), relative_blocks()
    small_abs = jnp.take(small_all, relative, axis=0).astype(F32)
    qv_all = small_abs[:, 6].reshape(2, 2, head_cols)
    qv_bias = lax.dynamic_index_in_dim(qv_all, core, 1, keepdims=False)
    up_all = small_abs[:, 7:9].reshape(n, 2, 2, rows).transpose(0, 2, 1, 3).reshape(2, hidden)
    up_bias = lax.dynamic_index_in_dim(up_all, core, 0, keepdims=False)

    def to_relative(array):
        blocks = array.reshape(array.shape[0], n, width)
        return jnp.take(blocks, absolute, axis=1).reshape(array.shape)

    def to_absolute(array):
        blocks = array.reshape(array.shape[0], n, width)
        return jnp.take(blocks, relative, axis=1).reshape(array.shape)

    length = lengths[0]
    own_ids = core * own_slots + jnp.arange(own_slots, dtype=jnp.int32)
    other_ids = (1 - core) * own_slots + jnp.arange(own_slots, dtype=jnp.int32)
    slot_ids = jnp.concatenate([own_ids, other_ids])
    key_valid = slot_ids < length
    row_valid = key_valid.astype(F32)[:, None]
    own_valid = row_valid[:own_slots]

    entering_all = with_other(to_relative(inputs[0])).astype(F32) * row_valid
    grad_low = with_other(to_relative(grad_out[0]))
    grad_res = grad_low[:own_slots].astype(F32)
    normal_one, scale_one = stats_of(entering_all)
    normed = (normal_one * gain_one + shift_one).astype(BF16)
    packed = jnp.dot(normed, qkv_full, preferred_element_type=F32)
    slots = 2 * own_slots
    heads = head_cols // HD
    head_shape = (slots, heads, HD)
    query = (packed[:, :head_cols] + qv_bias[0]).astype(BF16).reshape(head_shape)
    key = packed[:, head_cols : 2 * head_cols].astype(BF16).reshape(head_shape)
    value = (packed[:, 2 * head_cols :] + qv_bias[1]).astype(BF16).reshape(head_shape)
    score_scale = HD ** (-0.5)
    scores = jnp.einsum("qhd,khd->hqk", query, key, preferred_element_type=F32) * score_scale
    scores = jnp.where(key_valid[None, None, :], scores, MASK_FILL)
    raised = jnp.exp(scores - jnp.max(scores, axis=-1, keepdims=True))
    prob = raised / jnp.sum(raised, axis=-1, keepdims=True)
    prob_low = prob.astype(BF16)
    context = jnp.einsum("hqk,khd->qhd", prob_low, value, preferred_element_type=F32)
    context = context.astype(BF16).reshape(slots, head_cols)
    att_part = contract(context, proj_full, 1, 1)
    if cube:
        d_near, u_near_x, d_far_x, att_part = tie(d_near, u_near_x, d_far_x, att_part)
        d_near_x = flip(d_near, X_BIT)
        up_full = rows_of(u, u_far, u_near, u_x, u_far_x, u_near_x)
    attended = image_sum(att_part) + proj_bias
    entering = entering_all[:own_slots]
    middle = entering + attended
    normal_two, scale_two = stats_of(middle)
    normed_two = with_other((normal_two * gain_two + shift_two).astype(BF16))
    pre_act = jnp.dot(normed_two, up_full, preferred_element_type=F32) + up_bias
    cumulative = 0.5 * (1.0 + lax.erf(pre_act * ROOT_HALF))
    active = (pre_act * cumulative).astype(BF16)
    slope = cumulative + pre_act * (INV_ROOT_TWO_PI * jnp.exp(-0.5 * pre_act * pre_act))
    sum_down_bias = jnp.sum(grad_res, axis=0)
    if cube:
        d_near_x, active, slope = tie(d_near_x, active, slope)
        down_full = rows_of(d, d_far, d_near, d_x, d_far_x, d_near_x)
    grad_active = jnp.dot(grad_low, down_full, preferred_element_type=F32)
    grad_pre = (grad_active * slope).astype(BF16)
    gn_part = contract(grad_pre, up_full, 1, 1)
    if cube:
        down_low = sent_half(grad_low, active)
        gn_part, down_low, grad_pre = tie(gn_part, down_low, grad_pre)
        down_x = flip(down_low, X_BIT)
        up_low = sent_half(normed_two, grad_pre)
    grad_normed_two = image_sum(gn_part)
    grad_mid_part, sum_gain_two, sum_shift_two = norm_back(
        normal_two, scale_two, gain_two, grad_normed_two
    )
    grad_middle = grad_res + grad_mid_part
    grad_att_own = grad_middle.astype(BF16)
    sum_proj_bias = jnp.sum(grad_att_own.astype(F32), axis=0)
    grad_att = with_other(grad_att_own)
    if cube:
        down_x, up_low, grad_att, active = tie(down_x, up_low, grad_att, active)
        up_x = flip(up_low, X_BIT)
        down_two = kept_half(grad_low, active, down_x)
        down_near = flip(round_low(upper(down_two)), NEAR_BIT)
    branch = image_sum(contract(active, down_full, 1, 1)) + down_bias
    result = middle + branch
    output = to_absolute(result.astype(BF16))[None]
    square_sums = jnp.stack(
        [jnp.sum(own_valid * t * t) for t in (entering, attended, middle, branch, result)]
        + [jnp.sum(own_valid)]
    )
    sum_up_bias = jnp.sum(grad_pre.astype(F32), axis=0)
    grad_context = (
        jnp.dot(grad_att, proj_full, preferred_element_type=F32).astype(BF16).reshape(head_shape)
    )
    grad_prob = jnp.einsum("qhd,khd->hqk", grad_context, value, preferred_element_type=F32)
    grad_scores = (
        prob * (grad_prob - jnp.sum(prob * grad_prob, axis=-1, keepdims=True))
    ).astype(BF16)
    grad_query = jnp.einsum("hqk,khd->qhd", grad_scores, key, preferred_element_type=F32)
    grad_key = jnp.einsum("hqk,qhd->khd", grad_scores, query, preferred_element_type=F32)
    grad_value = jnp.einsum("hqk,qhd->khd", prob_low, grad_context, preferred_element_type=F32)
    grad_query = (grad_query * score_scale).astype(BF16).reshape(slots, head_cols)
    grad_key = (grad_key * score_scale).astype(BF16).reshape(slots, head_cols)
    grad_value = grad_value.astype(BF16).reshape(slots, head_cols)
    sum_qv_bias = jnp.concatenate(
        [jnp.sum(grad_query.astype(F32), axis=0), jnp.sum(grad_value.astype(F32), axis=0)]
    )
    grad_packed = jnp.concatenate([grad_query, grad_key, grad_value], axis=1)
    gn_one_part = contract(grad_packed, qkv_full, 1, 1)
    if cube:
        first_low = jnp.concatenate(
            [sent_half(normed, grad_packed), sent_half(grad_att, context)], axis=1
        )
        up_x, down_near, first_low, gn_one_part = tie(up_x, down_near, first_low, gn_one_part)
        first_x_high = flip(upper(first_low), X_BIT)
        up_two = kept_half(normed_two, grad_pre, up_x)
        up_near = flip(round_low(upper(up_two)), NEAR_BIT)
        down_one = lower(down_two) + down_near.astype(F32)
        down_far = flip(round_low(upper(down_one)), FAR_BIT)
        first_two = jnp.concatenate(
            [
                contract(normed[:, : D // 2], grad_packed, 0, 0),
                contract(grad_att[:, : D // 2], context, 0, 0),
            ],
            axis=1,
        )
        first_x_high, up_near, down_far, first_low = tie(
            first_x_high, up_near, down_far, first_low
        )
        first_x_low = flip(lower(first_low), X_BIT)
        first_near = flip(
            round_low(upper(first_two) + first_x_high.astype(F32)), NEAR_BIT
        )
        up_one = lower(up_two) + up_near.astype(F32)
        up_far = flip(round_low(upper(up_one)), FAR_BIT)
        sum_down = lower(down_one) + down_far.astype(F32)
        first_x_low, first_near, up_far = tie(first_x_low, first_near, up_far)
        first_one = lower(first_two) + first_x_low.astype(F32) + first_near.astype(F32)
        first_far = flip(round_low(upper(first_one)), FAR_BIT)
        sum_up = lower(up_one) + up_far.astype(F32)
        sum_first = lower(first_one) + first_far.astype(F32)
    else:
        sum_down = scatter_sum(contract(grad_low, active, 0, 0))
        sum_up = scatter_sum(contract(normed_two, grad_pre, 0, 0))
        sum_proj = scatter_sum(contract(grad_att, context, 0, 0))
        sum_qkv = scatter_sum(contract(normed, grad_packed, 0, 0))
        sum_first = jnp.concatenate([sum_qkv, sum_proj], axis=1)
    grad_normed = image_sum(gn_one_part)
    grad_enter, sum_gain_one, sum_shift_one = norm_back(
        normal_one[:own_slots], scale_one[:own_slots], gain_one, grad_normed
    )
    grad_inputs = to_absolute((grad_middle + grad_enter) * own_valid)[None]

    tail = jnp.concatenate(
        [sum_qv_bias, square_sums, jnp.zeros((D - 2 * head_cols - 6,), F32)]
    )
    per_core = jnp.stack(
        [
            sum_gain_one,
            sum_shift_one,
            sum_proj_bias,
            sum_gain_two,
            sum_shift_two,
            sum_down_bias,
            sum_up_bias.reshape(-1)[:D],
            tail,
        ]
    )
    if not is_cube():
        vectors_sum = lax.psum(per_core[:6], "fsdp")
        vector_sum = lax.dynamic_slice_in_dim(vectors_sum, place * width, width, 1)
        rest_sum = lax.psum(per_core[6:], "fsdp")
    else:
        total = per_core
        for bit, half in ((X_BIT, D // 2), (NEAR_BIT, D // 4), (FAR_BIT, D // 8)):
            arrived = flip(total, bit)
            vector_sum = total[:6, :half] + arrived[:6, half : 2 * half]
            rest_sum = total[6:] + arrived[6:]
            total = jnp.zeros((8, D), F32).at[:6, :half].set(vector_sum).at[6:].set(rest_sum)
    closing = jnp.zeros((8, D), F32).at[:6, :width].set(vector_sum).at[6:].set(rest_sum)
    other_closing = swap(closing, "ctx")
    vector_sum = vector_sum + other_closing[:6, :width]
    vector_own = lax.dynamic_slice_in_dim(vector_sum, core * rows, rows, 1)
    totals = (rest_sum[1] + other_closing[7])[2 * head_cols : 2 * head_cols + 6]
    rms = jnp.sqrt(totals[:5] / (totals[5] * D))
    qv_sum = by_core(
        rest_sum[1, : 2 * head_cols].reshape(2, 1, head_cols),
        other_closing[7, : 2 * head_cols].reshape(2, 1, head_cols),
        1,
    ).reshape(-1)
    qv_mine = lax.dynamic_slice_in_dim(qv_sum, (2 * place + core) * rows, rows, 0)
    up_sum = by_core(rest_sum[0], other_closing[6], 0)
    up_mine = lax.dynamic_slice_in_dim(up_sum, (2 * place + core) * 2 * rows, 2 * rows, 0)

    def owned(total):
        mine = lax.dynamic_slice_in_dim(total, core * rows, rows, 0)
        theirs = swap(lax.dynamic_slice_in_dim(total, (1 - core) * rows, rows, 0), "ctx")
        return mine, theirs

    mine, theirs = owned(sum_first)
    first_out = by_core(mine.reshape(rows, 4, 1, head_cols), theirs.reshape(rows, 4, 1, head_cols), 2)
    first_out = first_out.reshape(rows, 4, 2 * head_cols)
    grad_w_up = by_core(*owned(sum_up), 1)
    grad_w_down = by_core(*owned(sum_down), 1)
    return (
        output,
        grad_inputs,
        vector_own[0],
        vector_own[1],
        first_out[:, :3],
        qv_mine[:, None],
        first_out[:, 3],
        vector_own[2],
        vector_own[3],
        vector_own[4],
        grad_w_up,
        up_mine[:, None],
        grad_w_down,
        vector_own[5],
        rms,
    )


def solution(mesh):
    both = ("fsdp", "ctx")
    rows, vector, matrix = P("fsdp", "ctx", None), P(both), P(both, "tp")
    in_specs = (
        rows,
        P("fsdp"),
        rows,
        vector,
        vector,
        P(both, None, "tp"),
        matrix,
        matrix,
        vector,
        vector,
        vector,
        matrix,
        matrix,
        matrix,
        vector,
    )
    out_specs = (
        rows,
        rows,
        vector,
        vector,
        P(both, None, "tp"),
        matrix,
        matrix,
        vector,
        vector,
        vector,
        matrix,
        matrix,
        matrix,
        vector,
        P(),
    )
    return jax.shard_map(body, mesh=mesh, in_specs=in_specs, out_specs=out_specs, check_vma=False)
```

```python
import jax
import jax.numpy as jnp
from jax import lax
from jax.experimental import pallas as pl
from jax.experimental.pallas import tpu as pltpu
from jax.sharding import PartitionSpec as P

D = 1024
HD = 64
EPSILON = 1e-06
MASK_FILL = -1e30
ROOT_HALF = 0.7071067811865476
INV_ROOT_TWO_PI = 0.3989422804014327
F32 = jnp.float32
BF16 = jnp.bfloat16


def contract(left, right, left_dim, right_dim):
    return lax.dot_general(
        left, right, (((left_dim,), (right_dim,)), ((), ())), preferred_element_type=F32
    )


def round_low(values):
    return lax.reduce_precision(values, 8, 7).astype(BF16)


def swap(array, axis):
    return lax.ppermute(array, axis, [(0, 1), (1, 0)])


def flip(array, bit):
    n = lax.axis_size("fsdp")
    return lax.ppermute(array, "fsdp", [(i, i ^ bit) for i in range(n)])


X_BIT, NEAR_BIT, FAR_BIT = 1, 2, 4


def is_cube():
    return lax.axis_size("fsdp") == 8


def turned_bits(blocks):
    return (blocks % 2) * 4 + (blocks // 2 % 2) * 2 + blocks // 4


def relative_blocks():
    spots = jnp.arange(lax.axis_size("fsdp"), dtype=jnp.int32)
    if not is_cube():
        return spots
    return turned_bits(spots ^ lax.axis_index("fsdp"))


def absolute_places():
    blocks = jnp.arange(lax.axis_size("fsdp"), dtype=jnp.int32)
    if not is_cube():
        return blocks
    return turned_bits(blocks) ^ lax.axis_index("fsdp")


def tie(*values):
    return lax.optimization_barrier(values)


def rows_of(*pieces):
    return jnp.concatenate(pieces, axis=0)


def upper(array):
    return array[array.shape[0] // 2 :]


def lower(array):
    return array[: array.shape[0] // 2]


def scatter_sum(partial):
    low = round_low(partial)
    return lax.psum_scatter(low, "fsdp", scatter_dimension=0, tiled=True).astype(F32)


def low_cost():
    return pl.CostEstimate(flops=1000, transcendentals=0, bytes_accessed=1000)


def probabilities(query, key, mask):
    scores = contract(query, key, 1, 1) * (HD ** (-0.5))
    scores = jnp.where(mask > 0, scores, MASK_FILL)
    raised = jnp.exp(scores - jnp.max(scores, axis=-1, keepdims=True))
    return raised / jnp.sum(raised, axis=-1, keepdims=True)


def spans_of(pieces, block, pitch):
    spans, row = [], 0
    for index, piece in enumerate(pieces):
        for start in range(0, piece.shape[0], pitch):
            spans.append((index, start, row))
            row += block
    return spans


def merged(spans, block, pitch):
    if block != pitch:
        return [(index, start, row, block) for index, start, row in spans]
    joined = []
    for index, start, row in spans:
        if joined and joined[-1][0] == index:
            last = joined[-1]
            joined[-1] = (index, last[1], last[2], last[3] + block)
        else:
            joined.append((index, start, row, block))
    return joined


def times_pieces(left, pieces, spans, columns):
    total = None
    for index, start, row, size in spans:
        part = jnp.dot(
            left[:, row : row + size],
            pieces[index][start : start + size, columns],
            preferred_element_type=F32,
        )
        total = part if total is None else total + part
    return total


def times_pieces_back(left, pieces, spans, columns, own, other):
    half = own.shape[0]
    for index, start, row, size in spans:
        weight = pieces[index][start : start + size, columns]
        own[:, row : row + size] = contract(left[:half, :], weight, 1, 1)
        other[:, row : row + size] = contract(left[half:, :], weight, 1, 1).astype(BF16)


def shape_of(rows, columns, dtype):
    return jax.ShapeDtypeStruct((rows, columns), dtype)


def stacked(refs):
    return jnp.concatenate([ref[...] for ref in refs], axis=0)


def read_small(blocks, block, width, places_ref, relative, absolute):
    for index, (ref, start) in enumerate(blocks):
        lines = [
            ref[
                start + block + vector // 8 : start + block + vector // 8 + 1,
                vector % 8 * width : (vector % 8 + 1) * width,
            ]
            for vector in range(16)
        ]
        values = jnp.concatenate(lines, axis=0).astype(F32)
        relative[:, index * width : (index + 1) * width] = values
        to = pl.ds(pl.multiple_of(places_ref[index] * width, 128), width)
        absolute[:, to] = values


def attention(normal, vectors, bias, mask, pieces, block, pitch, places):
    slots, model = normal.shape
    width = pieces[0].shape[1] // 4
    half = slots // 2
    all_spans = spans_of(pieces, block, pitch)
    spans = merged(all_spans, block, pitch)
    given = [] if vectors is None else [vectors, bias]

    def kernel(places_ref, normal_ref, mask_ref, *refs):
        weights = refs[: len(pieces)]
        query, key, value, context, own, other, normed = refs[len(pieces) + len(given) :][:7]
        if given:
            small, own_bias = refs[len(pieces) : len(pieces) + 2]
            query_bias, value_bias = own_bias[0:1, :], own_bias[1:2, :]
        else:
            small, absolute = refs[-2:]
            blocks = [(weights[index], start) for index, start, _ in all_spans]
            read_small(blocks, block, model // len(blocks), places_ref, small, absolute)
            at = pl.multiple_of(places_ref[len(blocks)] * width, 128)
            query_bias = absolute[6:7, pl.ds(at, width)]
            value_bias = absolute[6:7, pl.ds(at + 2 * width, width)]
        normed[...] = (normal_ref[...] * small[0:1, :] + small[1:2, :]).astype(BF16)
        packed = times_pieces(normed, weights, spans, slice(0, 3 * width))
        query[...] = (packed[:, :width] + query_bias).astype(BF16)
        key[...] = packed[:, width : 2 * width].astype(BF16)
        value[...] = (packed[:, 2 * width :] + value_bias).astype(BF16)
        valid = mask_ref[...]
        parts = []
        for head in range(width // HD):
            at = slice(head * HD, (head + 1) * HD)
            prob = probabilities(query[:, at], key[:, at], valid)
            parts.append(jnp.dot(prob.astype(BF16), value[:, at], preferred_element_type=F32))
        context[...] = jnp.concatenate(parts, axis=1).astype(BF16)
        times_pieces_back(context, weights, spans, slice(3 * width, 4 * width), own, other)

    in_vmem = pl.BlockSpec(memory_space=pltpu.VMEM)
    small_shape = [] if given else [shape_of(16, model, F32)] * 2
    out_shape = (
        [shape_of(slots, width, BF16)] * 4
        + [shape_of(half, model, F32), shape_of(half, model, BF16), shape_of(slots, model, BF16)]
        + small_shape
    )
    return pl.pallas_call(
        kernel,
        name="attention",
        in_specs=[pl.BlockSpec(memory_space=pltpu.SMEM)]
        + [in_vmem] * (2 + len(pieces) + len(given)),
        out_specs=[in_vmem] * len(out_shape),
        out_shape=out_shape,
        cost_estimate=low_cost(),
    )(places, normal, mask, *pieces, *given)


def attention_back(grad_att, context, mask, query, key, value, pieces, block, pitch):
    slots, width = context.shape
    model = grad_att[0].shape[1]
    half = slots // 2
    scale = HD ** (-0.5)
    spans = merged(spans_of(pieces, block, pitch), block, pitch)

    def kernel(grad_own, grad_other, context_ref, mask_ref, query_ref, key_ref, value_ref, *refs):
        weights = refs[: len(pieces)]
        packed_own, packed_other, own, other, bias_sum, packed = refs[len(pieces) :]
        grad_ref = stacked((grad_own, grad_other))
        valid = mask_ref[...]
        grad_context = times_pieces(
            grad_ref, weights, spans, slice(3 * width, 4 * width)
        ).astype(BF16)
        queries, keys, values = [], [], []
        for head in range(width // HD):
            at = slice(head * HD, (head + 1) * HD)
            q, k, v, g = query_ref[:, at], key_ref[:, at], value_ref[:, at], grad_context[:, at]
            prob = probabilities(q, k, valid)
            grad_prob = contract(g, v, 1, 1)
            dots = jnp.sum(prob * grad_prob, axis=-1, keepdims=True)
            grad_scores = (prob * (grad_prob - dots)).astype(BF16)
            queries.append(jnp.dot(grad_scores, k, preferred_element_type=F32) * scale)
            keys.append(contract(grad_scores, q, 0, 0) * scale)
            values.append(contract(prob.astype(BF16), g, 0, 0))
        for kind, parts in enumerate((queries, keys, values)):
            joined = jnp.concatenate(parts, axis=1).astype(BF16)
            packed[:, kind * width : (kind + 1) * width] = joined
            if kind != 1:
                at = (kind // 2) * width
                bias_sum[:, at : at + width] = jnp.sum(joined.astype(F32), axis=0, keepdims=True)
        packed[:, 3 * width :] = context_ref[...]
        packed_own[...] = packed[:half, :]
        packed_other[...] = packed[half:, :]
        grads = packed.at[:, : 3 * width]
        times_pieces_back(grads, weights, spans, slice(0, 3 * width), own, other)

    return pl.pallas_call(
        kernel,
        name="attention_back",
        out_shape=[
            shape_of(half, 4 * width, BF16),
            shape_of(half, 4 * width, BF16),
            shape_of(half, model, F32),
            shape_of(half, model, BF16),
            shape_of(1, 2 * width, F32),
        ],
        scratch_shapes=[pltpu.VMEM((slots, 4 * width), BF16)],
        cost_estimate=low_cost(),
    )(*grad_att, context, mask, query, key, value, *pieces)


def hidden_layer(own, other, normed, bias, pieces, block):
    half, model = own.shape
    slots, hidden = 2 * half, bias.shape[1]
    spans = merged(spans_of(pieces, block, block), block, block)

    def kernel(own_ref, other_ref, normed_ref, bias_ref, *refs):
        message, slope = refs[len(pieces) :]
        left = stacked((own_ref, other_ref))
        pre_act = times_pieces(left, refs[: len(pieces)], spans, slice(0, hidden))
        pre_act = pre_act + bias_ref[...]
        cumulative = 0.5 * (1.0 + lax.erf(pre_act * ROOT_HALF))
        message[:slots, :] = (pre_act * cumulative).astype(BF16)
        message[slots:, : model // 2] = normed_ref[:half, model // 2 :]
        message[slots:, model // 2 :] = own_ref[:, model // 2 :]
        slope[...] = cumulative + pre_act * (
            INV_ROOT_TWO_PI * jnp.exp(-0.5 * pre_act * pre_act)
        )

    return pl.pallas_call(
        kernel,
        name="hidden_layer",
        out_shape=[shape_of(slots + half, hidden, BF16), shape_of(slots, hidden, F32)],
        cost_estimate=low_cost(),
    )(own, other, normed, bias, *pieces)


def hidden_back(grads, slope, up_pieces, down_pieces, block):
    model = grads[0].shape[1]
    slots, hidden = slope.shape
    half = slots // 2
    spans = merged(spans_of(up_pieces, block, block), block, block)
    down_spans = merged(spans_of(down_pieces, block, block), block, block)
    count = len(up_pieces)
    total = count + len(down_pieces)

    def kernel(grad_own, grad_other, slope_ref, *refs):
        grad_ref = stacked((grad_own, grad_other))
        up, down = refs[:count], refs[count:total]
        grad_pre, own, other, bias_sum = refs[total:]
        grad_active = times_pieces(grad_ref, down, down_spans, slice(0, hidden))
        low = (grad_active * slope_ref[...]).astype(BF16)
        grad_pre[...] = low
        bias_sum[...] = jnp.sum(low.astype(F32), axis=0, keepdims=True)
        times_pieces_back(grad_pre, up, spans, slice(0, hidden), own, other)

    return pl.pallas_call(
        kernel,
        name="hidden_back",
        out_shape=[
            shape_of(slots, hidden, BF16),
            shape_of(half, model, F32),
            shape_of(half, model, BF16),
            shape_of(1, hidden, F32),
        ],
        cost_estimate=low_cost(),
    )(*grads, slope, *up_pieces, *down_pieces)


def project_back(values, slots, pieces, block):
    columns = values.shape[1]
    spans = merged(spans_of(pieces, block, block), block, block)
    half = slots // 2

    def kernel(values_ref, *refs):
        left = values_ref.at[:slots, :]
        times_pieces_back(left, refs[: len(pieces)], spans, slice(0, columns), refs[-2], refs[-1])

    return pl.pallas_call(
        kernel,
        name="project_back",
        out_shape=[shape_of(half, D, F32), shape_of(half, D, BF16)],
        cost_estimate=low_cost(),
    )(values, *pieces)


def weight_grad(groups, rights, parts):
    columns = rights[0][0].shape[1]
    cut = D // 4
    arrays, index_of = [], {}

    def index(array):
        if id(array) not in index_of:
            index_of[id(array)] = len(arrays)
            arrays.append(array)
        return index_of[id(array)]

    right_rows = [(index(array), row, count) for array, row, count in rights]
    left_rows = [
        ([(index(array), row, count, column) for array, row, count, column in lefts], lo, hi)
        for lefts, lo, hi in groups
    ]
    size = cut // parts

    def kernel(*refs):
        outs = refs[len(arrays) :]
        targets = [(outs[part], cut + part * size) for part in range(parts)] + [(outs[-1], 0)]
        for lefts, lo, hi in left_rows:
            right = jnp.concatenate(
                [refs[at][row : row + count, lo:hi] for at, row, count in right_rows], axis=0
            )
            for target, first in targets:
                left = jnp.concatenate(
                    [
                        refs[at][row : row + count, column + first : column + first + target.shape[0]]
                        for at, row, count, column in lefts
                    ],
                    axis=0,
                )
                target[:, lo:hi] = contract(left, right, 0, 0).astype(target.dtype)

    return pl.pallas_call(
        kernel,
        name="weight_grad",
        out_shape=[shape_of(size, columns, BF16)] * parts + [shape_of(cut, columns, F32)],
        cost_estimate=low_cost(),
    )(*arrays)


def norm_of(values):
    mean = jnp.mean(values, axis=-1, keepdims=True)
    centered = values - mean
    scale = lax.rsqrt(jnp.mean(centered * centered, axis=-1, keepdims=True) + EPSILON)
    return centered * scale, scale


def valid_rows(rows, places_ref):
    slot = lax.broadcasted_iota(jnp.int32, (rows, 1), 0) + places_ref[places_ref.shape[0] - 2]
    return (slot < places_ref[places_ref.shape[0] - 1]).astype(F32)


def assemble(mine, theirs, places):
    rows, columns = mine.shape
    width = columns // 4
    last = places.shape[0] - 3

    def kernel(places_ref, mine_ref, theirs_ref, three, fourth):
        core = places_ref[last]
        for source, half in ((mine_ref, core), (theirs_ref, 1 - core)):
            to = pl.ds(pl.multiple_of(half * width, 128), width)
            for kind in range(3):
                three[:, kind, to] = source[:, kind * width : (kind + 1) * width]
            fourth[:, to] = source[:, 3 * width :]

    in_vmem = pl.BlockSpec(memory_space=pltpu.VMEM)
    return pl.pallas_call(
        kernel,
        name="assemble",
        in_specs=[pl.BlockSpec(memory_space=pltpu.SMEM)] + [in_vmem] * 2,
        out_specs=[in_vmem] * 2,
        out_shape=[
            jax.ShapeDtypeStruct((rows, 3, 2 * width), F32),
            shape_of(rows, 2 * width, F32),
        ],
        cost_estimate=low_cost(),
    )(places, mine, theirs)


def norm_grad(normal, scale, gain, grad):
    weighted = grad * gain
    return scale * (
        weighted
        - jnp.mean(weighted, axis=-1, keepdims=True)
        - normal * jnp.mean(weighted * normal, axis=-1, keepdims=True)
    )


def column_sum(values):
    return jnp.sum(values, axis=0, keepdims=True)


def second_norm_back(middle, gain, low, other_low, grad_res):
    rows, model = middle.shape

    def kernel(middle_ref, gain_ref, low_ref, other_ref, res_ref, *outs):
        grad_middle, grad_att, sums = outs
        grad = low_ref[...].astype(F32) + other_ref[...].astype(F32)
        res = res_ref[...].astype(F32)
        n, scale = norm_of(middle_ref[...])
        total = res + norm_grad(n, scale, gain_ref[...], grad)
        grad_middle[...] = total
        rounded = total.astype(BF16)
        grad_att[...] = rounded
        sums[0:1, :] = column_sum(rounded.astype(F32))
        sums[1:2, :] = column_sum(grad * n)
        sums[2:3, :] = column_sum(grad)
        sums[3:4, :] = column_sum(res)

    return pl.pallas_call(
        kernel,
        name="second_norm_back",
        out_shape=[
            shape_of(rows, model, F32),
            shape_of(rows, model, BF16),
            shape_of(4, model, F32),
        ],
        cost_estimate=low_cost(),
    )(middle, gain, low, other_low, grad_res)


def place_blocks(target, rows, values, places_ref):
    count = places_ref.shape[0] - 3
    width = values.shape[1] // count
    if width % 128:
        target[rows, :] = values
        return
    for block in range(count):
        to = pl.ds(pl.multiple_of(places_ref[block] * width, 128), width)
        target[rows, to] = values[:, block * width : (block + 1) * width]


def finish(middle, entering, attended, low, other_low, bias, places):
    rows, model = middle.shape

    def kernel(
        places_ref, middle_ref, entering_ref, attended_ref, low_ref, other_ref, bias_ref,
        output, stats
    ):
        branch = low_ref[...].astype(F32) + other_ref[...].astype(F32) + bias_ref[...]
        result = middle_ref[...] + branch
        place_blocks(output, slice(None), result.astype(BF16), places_ref)
        good = valid_rows(rows, places_ref)
        lane = lax.broadcasted_iota(jnp.int32, (1, 128), 1)
        row = jnp.where(lane == 5, column_sum(good), 0.0)
        terms = (entering_ref[...], attended_ref[...], middle_ref[...], branch, result)
        for index, term in enumerate(terms):
            total = jnp.sum(column_sum(term * term * good), axis=1, keepdims=True)
            row = jnp.where(lane == index, total, row)
        stats[...] = row

    in_vmem = pl.BlockSpec(memory_space=pltpu.VMEM)
    return pl.pallas_call(
        kernel,
        name="finish",
        in_specs=[pl.BlockSpec(memory_space=pltpu.SMEM)] + [in_vmem] * 6,
        out_specs=[in_vmem] * 2,
        out_shape=[shape_of(rows, model, BF16), shape_of(1, 128, F32)],
        cost_estimate=low_cost(),
    )(places, middle, entering, attended, low, other_low, bias)


def first_norm_back(
    inputs, gain, low, other_low, grad_middle, sums, up_sum, qv_sum, stats, places
):
    rows, model = inputs.shape

    def kernel(
        places_ref, inputs_ref, gain_ref, low_ref, other_ref, middle_ref,
        sums_ref, up_ref, qv_ref, stats_ref, grad_inputs, message
    ):
        grad = low_ref[...].astype(F32) + other_ref[...].astype(F32)
        valid = valid_rows(rows, places_ref)
        n, scale = norm_of(inputs_ref[...].astype(F32) * valid)
        total = middle_ref[...] + norm_grad(n, scale, gain_ref[...], grad)
        total = total * valid
        vectors = jnp.concatenate(
            [column_sum(grad * n), column_sum(grad), sums_ref[...]], axis=0
        )
        message[6:7, :] = up_ref[...]
        message[7:8, :] = jnp.zeros((1, model), F32)
        message[7:8, : qv_ref.shape[1]] = qv_ref[...]
        message[7:8, model - 128 :] = stats_ref[...]
        place_blocks(grad_inputs, slice(None), total, places_ref)
        place_blocks(message, slice(0, 6), vectors, places_ref)

    in_vmem = pl.BlockSpec(memory_space=pltpu.VMEM)
    return pl.pallas_call(
        kernel,
        name="first_norm_back",
        in_specs=[pl.BlockSpec(memory_space=pltpu.SMEM)] + [in_vmem] * 9,
        out_specs=[in_vmem] * 2,
        out_shape=[shape_of(rows, model, F32), shape_of(8, model, F32)],
        cost_estimate=low_cost(),
    )(
        places, inputs, gain, low, other_low, grad_middle, sums, up_sum, qv_sum, stats
    )


def halves_low(own, other):
    low = round_low(own + swap(other, "ctx").astype(F32))
    return low, swap(low, "tp")


def halves_sum(own, other):
    low = round_low(own + swap(other, "ctx").astype(F32))
    return low.astype(F32) + swap(low, "tp").astype(F32)


def coded(values):
    high = lax.reduce_precision(values, 8, 7)
    return rows_of(high.astype(BF16), round_low(values - high))


def decoded(rows):
    return lower(rows).astype(F32) + upper(rows).astype(F32)


def with_other(own):
    return jnp.concatenate([own, swap(own, "ctx")], axis=0)


def body(
    inputs,
    lengths,
    grad_out,
    ln1_gain,
    ln1_shift,
    w_qkv,
    b_qv,
    w_proj,
    b_proj,
    ln2_gain,
    ln2_shift,
    w_up,
    b_up,
    w_down,
    b_down,
):
    n = lax.axis_size("fsdp")
    cube = is_cube()
    core = lax.axis_index("ctx")
    place = lax.axis_index("fsdp")
    rows = w_up.shape[0]
    head_cols = w_proj.shape[1] // 2
    hidden = w_up.shape[1] // 2
    own_slots = inputs.shape[1]
    width = D // n

    qkv_halves = w_qkv.reshape(rows, 3, 2, head_cols)
    proj_halves = w_proj.reshape(rows, 2, head_cols)
    up_halves = w_up.reshape(rows, 2, hidden)
    down_halves = w_down.reshape(rows, 2, hidden)

    def first_half(which):
        return jnp.concatenate(
            [
                lax.dynamic_index_in_dim(qkv_halves, which, 2, keepdims=False).reshape(
                    rows, 3 * head_cols
                ),
                lax.dynamic_index_in_dim(proj_halves, which, 1, keepdims=False),
            ],
            axis=1,
        )

    def half_of(halves, which):
        return lax.dynamic_index_in_dim(halves, which, 1, keepdims=False)

    def by_core(own, other, axis):
        return jnp.where(
            core == 0,
            jnp.concatenate([own, other], axis=axis),
            jnp.concatenate([other, own], axis=axis),
        )

    small = jnp.concatenate(
        [
            jnp.stack([ln1_gain, ln1_shift, b_proj, ln2_gain, ln2_shift, b_down, b_qv[:, 0]]),
            b_up.reshape(2, rows),
        ]
    )
    small_both = by_core(small, swap(small, "ctx"), 1)
    first_own, first_other = first_half(core), first_half(1 - core)
    first_mine = by_core(first_own, swap(first_other, "ctx"), 0)
    small_flat = jnp.zeros((16 * 2 * rows,), BF16)
    small_flat = small_flat.at[: 9 * 2 * rows].set(small_both.reshape(-1))
    cols = first_mine.shape[1]
    small_rows = -(-16 * 2 * rows // cols)
    small_rows_padded = -(-small_rows // 8) * 8
    small_block = jnp.zeros((small_rows_padded * cols,), BF16)
    small_block = small_block.at[: 16 * 2 * rows].set(small_flat).reshape(small_rows_padded, cols)

    first_shard = jnp.concatenate([first_mine, small_block], axis=0)
    first_shard, inputs, grad_out, up_halves, down_halves = tie(
        first_shard, inputs, grad_out, up_halves, down_halves
    )
    u, d = (
        by_core(half_of(t, core), swap(half_of(t, 1 - core), "ctx"), 0)
        for t in (up_halves, down_halves)
    )
    absolute, relative = absolute_places(), relative_blocks()

    def to_relative(array):
        blocks = array.reshape(array.shape[0], n, width)
        return jnp.take(blocks, absolute, axis=1).reshape(array.shape)

    grad_own = to_relative(grad_out[0])
    f = first_shard
    if cube:
        f_far, f_x = flip(f, FAR_BIT), flip(f, X_BIT)
        grad_far = flip(grad_own[:, D // 2 :], X_BIT)
        f_far, f_x, grad_far, u, d = tie(f_far, f_x, grad_far, u, d)
        u_x = flip(u, X_BIT)
        f_near = flip(rows_of(f, f_far), NEAR_BIT)
        u_far, f_far_x, d_x = flip(u, FAR_BIT), flip(f_far, X_BIT), flip(d, X_BIT)
        f_near, u_far, f_far_x, u_x, d_x, u, d = tie(f_near, u_far, f_far_x, u_x, d_x, u, d)
        u_near = flip(rows_of(u, u_far), NEAR_BIT)
        d_far, f_near_x, u_far_x = flip(d, FAR_BIT), flip(f_near, X_BIT), flip(u_far, X_BIT)
        d_far, f_near_x, u_far_x, u_near, d = tie(d_far, f_near_x, u_far_x, u_near, d)
        d_near = flip(rows_of(d, d_far), NEAR_BIT)
        u_near_x, d_far_x = flip(u_near, X_BIT), flip(d_far, X_BIT)
        first_pieces = [f, f_far, f_near, f_x, f_far_x, f_near_x]
    else:
        first_pieces, up_pieces, down_pieces = (
            [lax.all_gather(t, "fsdp", tiled=True)] for t in (f, u, d)
        )
    block, pitch = 2 * rows, 2 * rows + small_rows_padded
    vectors = qv_bias = None
    if not cube:
        whole = first_pieces[0].reshape(n, pitch, cols)
        first_pieces, pitch = [whole[:, :block].reshape(D, cols)], block
        small_abs = whole[:, block:].reshape(n, -1)[:, : 16 * 2 * rows]
        small_abs = small_abs.reshape(n, 16, 2 * rows).astype(F32)
        vectors = small_abs.transpose(1, 0, 2).reshape(16, D)
        qv_all = small_abs[:, 6].reshape(2, 2, head_cols)
        qv_bias = lax.dynamic_index_in_dim(qv_all, core, 1, keepdims=False)

    length = lengths[0]
    own_ids = core * own_slots + jnp.arange(own_slots, dtype=jnp.int32)
    other_ids = (1 - core) * own_slots + jnp.arange(own_slots, dtype=jnp.int32)
    slot_ids = jnp.concatenate([own_ids, other_ids])
    key_valid = slot_ids < length
    row_valid = key_valid.astype(F32)[:, None]
    places = jnp.concatenate([absolute, jnp.stack([core, core * own_slots, length])])

    inputs_own = to_relative(inputs[0])
    entering_all = with_other(inputs_own).astype(F32) * row_valid
    grads = (grad_own, swap(grad_own, "ctx"))
    normal_one, _ = norm_of(entering_all)
    slots = 2 * own_slots
    key_mask = row_valid.reshape(1, slots)
    query, key, value, context, att_own, att_other, normed, *found = attention(
        normal_one, vectors, qv_bias, key_mask, first_pieces, block, pitch, places
    )
    if cube:
        vectors, vectors_abs = found
        small_abs = vectors_abs.reshape(16, n, 2 * rows).transpose(1, 0, 2)
    gain_one, _, proj_bias, gain_two, shift_two, down_bias = (vectors[i] for i in range(6))
    up_all = small_abs[:, 7:9].reshape(n, 2, 2, rows).transpose(0, 2, 1, 3).reshape(2, hidden)
    up_bias = lax.dynamic_index_in_dim(up_all, core, 0, keepdims=False)
    if cube:
        d_near, u_near_x, d_far_x, att_own, att_other = tie(
            d_near, u_near_x, d_far_x, att_own, att_other
        )
        d_near_x = flip(lower(d_near), X_BIT)
        up_pieces = [u, u_far, u_near, u_x, u_far_x, u_near_x]
    att_low, att_tp = halves_low(att_own, att_other)
    if cube:
        att_low, att_tp, d_near_x, d_near = tie(att_low, att_tp, d_near_x, d_near)
        d_last_x = flip(upper(d_near), X_BIT)
    attended = att_low.astype(F32) + att_tp.astype(F32) + proj_bias
    entering = entering_all[:own_slots]
    middle = entering + attended
    normal_two, _ = norm_of(middle)
    normed_two_own = (normal_two * gain_two + shift_two).astype(BF16)
    normed_two_other = swap(normed_two_own, "ctx")
    active, slope = hidden_layer(
        normed_two_own, normed_two_other, normed, up_bias[None], up_pieces, block
    )
    if cube:
        active, slope, d_last_x = tie(active, slope, d_last_x)
        active_far = flip(active, X_BIT)
        down_pieces = [d, d_far, d_near, d_x, d_far_x, d_near_x, d_last_x]
    grad_pre, gn_own, gn_other, sum_up_bias = hidden_back(
        grads, slope, up_pieces, down_pieces, block
    )
    gn_low = round_low(gn_own + swap(gn_other, "ctx").astype(F32))
    if cube:
        gn_low, active = tie(gn_low, active)
    gn_tp = swap(gn_low, "tp")
    branch_own, branch_other = project_back(active, slots, down_pieces, block)
    if cube:
        gn_low, gn_tp, active_far, grad_pre, branch_own, branch_other = tie(
            gn_low, gn_tp, active_far, grad_pre, branch_own, branch_other
        )
        pre_far = flip(grad_pre, X_BIT)
        size, half = own_slots, D // 2
    grad_middle, grad_att_own, sums = second_norm_back(
        middle, gain_two[None], gn_low, gn_tp, grad_own
    )
    if cube:
        grad_att_own, active_far, branch_own, branch_other = tie(
            grad_att_own, active_far, branch_own, branch_other
        )
        att_far = flip(grad_att_own[:, half:], X_BIT)
        down_high, down_two = weight_grad(
            [
                (
                    [(t, 0, size, 0) for t in (*grads, grad_far, swap(grad_far, "ctx"))],
                    0,
                    hidden,
                )
            ],
            [(active, 0, slots), (active_far, 0, slots)],
            1,
        )
    grad_att_other = swap(grad_att_own, "ctx")
    if cube:
        down_high, grad_att_other = tie(down_high, grad_att_other)
        down_near = flip(down_high, NEAR_BIT)
    branch_low, branch_tp = halves_low(branch_own, branch_other)
    packed, packed_other, gn_one_own, gn_one_other, sum_qv_bias = attention_back(
        (grad_att_own, grad_att_other), context, key_mask, query, key, value, first_pieces, block, pitch
    )
    if cube:
        pre_far, att_far, down_near, packed, gn_one_own, gn_one_other, branch_low, branch_tp = tie(
            pre_far, att_far, down_near, packed, gn_one_own, gn_one_other, branch_low, branch_tp
        )
        packed_one = flip(packed, X_BIT)
        down_far = flip(round_low(upper(down_two) + upper(down_near).astype(F32)), FAR_BIT)
        normed_swapped = swap(active_far[slots:], "ctx")
        up_high, up_two = weight_grad(
            [
                (
                    [
                        (normed_two_own, 0, size, 0),
                        (normed_two_other, 0, size, 0),
                        (active_far, slots, size, half),
                        (normed_swapped, 0, size, half),
                    ],
                    0,
                    hidden,
                )
            ],
            [(grad_pre, 0, slots), (pre_far, 0, slots)],
            1,
        )
    gn_one_low = round_low(gn_one_own + swap(gn_one_other, "ctx").astype(F32))
    if cube:
        gn_one_low, packed_one, up_high, packed_other, down_far = tie(
            gn_one_low, packed_one, up_high, packed_other, down_far
        )
        packed_two = flip(packed_other, X_BIT)
        up_near = flip(up_high, NEAR_BIT)
    gn_one_tp = swap(gn_one_low, "tp")
    if cube:
        att_swapped = swap(att_far, "ctx")
        packed_two, gn_one_tp, att_swapped = tie(packed_two, gn_one_tp, att_swapped)
        *first_high, first_two = weight_grad(
            [
                (
                    [
                        (normed, 0, slots, 0),
                        (active_far, slots, size, 0),
                        (normed_swapped, 0, size, 0),
                    ],
                    0,
                    3 * head_cols,
                ),
                (
                    [
                        (t, 0, size, 0)
                        for t in (grad_att_own, grad_att_other, att_far, att_swapped)
                    ],
                    3 * head_cols,
                    4 * head_cols,
                ),
            ],
            [(t, 0, size) for t in (packed, packed_other, packed_one, packed_two)],
            2,
        )
    else:
        packed = rows_of(packed, packed_other)
        sum_down = scatter_sum(contract(rows_of(*grads), active[:slots], 0, 0))
        sum_up = scatter_sum(contract(rows_of(normed_two_own, normed_two_other), grad_pre, 0, 0))
        sum_first = jnp.concatenate(
            [
                scatter_sum(contract(normed, packed[:, : 3 * head_cols], 0, 0)),
                scatter_sum(
                    contract(rows_of(grad_att_own, grad_att_other), context, 0, 0)
                ),
            ],
            axis=1,
        )
    output, stats = finish(
        middle, entering, attended, branch_low, branch_tp, down_bias[None], places
    )
    output = output[None]
    grad_inputs, message = first_norm_back(
        inputs_own,
        gain_one[None],
        gn_one_low,
        gn_one_tp,
        grad_middle,
        sums,
        sum_up_bias,
        sum_qv_bias,
        stats,
        places,
    )
    grad_inputs = grad_inputs[None]

    if cube:
        message = message + flip(message, X_BIT)
        first_high, up_near, message = tie(first_high, up_near, message)
        first_near = [flip(rows_of(first_high[1], coded(message)), NEAR_BIT)]
        up_far = flip(round_low(upper(up_two) + upper(up_near).astype(F32)), FAR_BIT)
        sum_down = lower(down_two) + lower(down_near).astype(F32) + down_far.astype(F32)
        first_near[0], first_high, up_far = tie(first_near[0], first_high, up_far)
        first_near.append(flip(first_high[0], NEAR_BIT))
        message = message + decoded(first_near[0][block:])
        first_low = round_low(upper(first_two) + first_near[0][:block].astype(F32))
        first_far = flip(rows_of(first_low, coded(message)), FAR_BIT)
        first_near[1], first_far = tie(first_near[1], first_far)
        sum_first = (
            lower(first_two) + first_near[1].astype(F32) + first_far[:block].astype(F32)
        )
        sum_up = lower(up_two) + lower(up_near).astype(F32) + up_far.astype(F32)
        message = message + decoded(first_far[block:])
    else:
        message = lax.psum(message, "fsdp")
    other_message = swap(message, "ctx")
    at = 2 * place + core
    vector_own = lax.dynamic_slice_in_dim(
        message[:6] + other_message[:6], at * rows, rows, 1
    )
    totals = (message[7] + other_message[7])[D - 128 : D - 122]
    rms = jnp.sqrt(totals[:5] / (totals[5] * D))
    qv_sum = by_core(
        message[7, : 2 * head_cols].reshape(2, 1, head_cols),
        other_message[7, : 2 * head_cols].reshape(2, 1, head_cols),
        1,
    ).reshape(-1)
    qv_mine = lax.dynamic_slice_in_dim(qv_sum, at * rows, rows, 0)
    up_sum = by_core(message[6], other_message[6], 0)
    up_mine = lax.dynamic_slice_in_dim(up_sum, at * 2 * rows, 2 * rows, 0)

    def owned(total):
        mine = lax.dynamic_slice_in_dim(total, core * rows, rows, 0)
        theirs = swap(lax.dynamic_slice_in_dim(total, (1 - core) * rows, rows, 0), "ctx")
        return mine, theirs

    grad_w_qkv, grad_w_proj = assemble(*owned(sum_first), places)
    grad_w_up = by_core(*owned(sum_up), 1)
    grad_w_down = by_core(*owned(sum_down), 1)
    return (
        output,
        grad_inputs,
        vector_own[0],
        vector_own[1],
        grad_w_qkv,
        qv_mine[:, None],
        grad_w_proj,
        vector_own[2],
        vector_own[3],
        vector_own[4],
        grad_w_up,
        up_mine[:, None],
        grad_w_down,
        vector_own[5],
        rms,
    )


def solution(mesh):
    both = ("fsdp", "ctx")
    rows, vector, matrix = P("fsdp", "ctx", None), P(both), P(both, "tp")
    in_specs = (
        rows,
        P("fsdp"),
        rows,
        vector,
        vector,
        P(both, None, "tp"),
        matrix,
        matrix,
        vector,
        vector,
        vector,
        matrix,
        matrix,
        matrix,
        vector,
    )
    out_specs = (
        rows,
        rows,
        vector,
        vector,
        P(both, None, "tp"),
        matrix,
        matrix,
        vector,
        vector,
        vector,
        matrix,
        matrix,
        matrix,
        vector,
        P(),
    )
    return jax.shard_map(body, mesh=mesh, in_specs=in_specs, out_specs=out_specs, check_vma=False)
```

```python
import jax
import jax.numpy as jnp
from jax import lax
from jax.experimental import pallas as pl
from jax.experimental.pallas import tpu as pltpu
from jax.sharding import PartitionSpec as P

D = 1024
HD = 64
EPSILON = 1e-06
MASK_FILL = -1e30
ROOT_HALF = 0.7071067811865476
INV_ROOT_TWO_PI = 0.3989422804014327
F32 = jnp.float32
BF16 = jnp.bfloat16


def contract(left, right, left_dim, right_dim):
    return lax.dot_general(
        left, right, (((left_dim,), (right_dim,)), ((), ())), preferred_element_type=F32
    )


def round_low(values):
    return lax.reduce_precision(values, 8, 7).astype(BF16)


def swap(array, axis):
    return lax.ppermute(array, axis, [(0, 1), (1, 0)])


def flip(array, bit):
    n = lax.axis_size("fsdp")
    return lax.ppermute(array, "fsdp", [(i, i ^ bit) for i in range(n)])


X_BIT, NEAR_BIT, FAR_BIT = 1, 2, 4


def is_cube():
    return lax.axis_size("fsdp") == 8


def turned_bits(blocks):
    return (blocks % 2) * 4 + (blocks // 2 % 2) * 2 + blocks // 4


def relative_blocks():
    spots = jnp.arange(lax.axis_size("fsdp"), dtype=jnp.int32)
    if not is_cube():
        return spots
    return turned_bits(spots ^ lax.axis_index("fsdp"))


def absolute_places():
    blocks = jnp.arange(lax.axis_size("fsdp"), dtype=jnp.int32)
    if not is_cube():
        return blocks
    return turned_bits(blocks) ^ lax.axis_index("fsdp")


def tie(*values):
    return lax.optimization_barrier(values)


def rows_of(*pieces):
    return jnp.concatenate(pieces, axis=0)


def upper(array):
    return array[array.shape[0] // 2 :]


def lower(array):
    return array[: array.shape[0] // 2]


def scatter_sum(partial):
    low = round_low(partial)
    return lax.psum_scatter(low, "fsdp", scatter_dimension=0, tiled=True).astype(F32)


def low_cost():
    return pl.CostEstimate(flops=1000, transcendentals=0, bytes_accessed=1000)


def probabilities(query, key, mask):
    scores = contract(query, key, 1, 1) * (HD ** (-0.5))
    scores = jnp.where(mask > 0, scores, MASK_FILL)
    raised = jnp.exp(scores - jnp.max(scores, axis=-1, keepdims=True))
    return raised / jnp.sum(raised, axis=-1, keepdims=True)


def spans_of(pieces, block, pitch):
    spans, row = [], 0
    for index, piece in enumerate(pieces):
        for start in range(0, piece.shape[0], pitch):
            spans.append((index, start, row))
            row += block
    return spans


def merged(spans, block, pitch):
    if block != pitch:
        return [(index, start, row, block) for index, start, row in spans]
    joined = []
    for index, start, row in spans:
        if joined and joined[-1][0] == index:
            last = joined[-1]
            joined[-1] = (index, last[1], last[2], last[3] + block)
        else:
            joined.append((index, start, row, block))
    return joined


def times_pieces(left, pieces, spans, columns):
    total = None
    for index, start, row, size in spans:
        part = jnp.dot(
            left[:, row : row + size],
            pieces[index][start : start + size, columns],
            preferred_element_type=F32,
        )
        total = part if total is None else total + part
    return total


def times_pieces_back(left, pieces, spans, columns, own, other):
    half = own.shape[0]
    for index, start, row, size in spans:
        weight = pieces[index][start : start + size, columns]
        own[:, row : row + size] = contract(left[:half, :], weight, 1, 1)
        other[:, row : row + size] = contract(left[half:, :], weight, 1, 1).astype(BF16)


def shape_of(rows, columns, dtype):
    return jax.ShapeDtypeStruct((rows, columns), dtype)


def stacked(refs):
    return jnp.concatenate([ref[...] for ref in refs], axis=0)


def read_small(blocks, block, width, places_ref, relative, absolute):
    for index, (ref, start) in enumerate(blocks):
        lines = [
            ref[
                start + block + vector // 8 : start + block + vector // 8 + 1,
                vector % 8 * width : (vector % 8 + 1) * width,
            ]
            for vector in range(16)
        ]
        values = jnp.concatenate(lines, axis=0).astype(F32)
        relative[:, index * width : (index + 1) * width] = values
        to = pl.ds(pl.multiple_of(places_ref[index] * width, 128), width)
        absolute[:, to] = values


def attention(normal, vectors, bias, mask, pieces, block, pitch, places):
    slots, model = normal.shape
    width = pieces[0].shape[1] // 4
    half = slots // 2
    all_spans = spans_of(pieces, block, pitch)
    spans = merged(all_spans, block, pitch)
    given = [] if vectors is None else [vectors, bias]

    def kernel(places_ref, normal_ref, mask_ref, *refs):
        weights = refs[: len(pieces)]
        query, key, value, context, own, other, normed = refs[len(pieces) + len(given) :][:7]
        if given:
            small, own_bias = refs[len(pieces) : len(pieces) + 2]
            query_bias, value_bias = own_bias[0:1, :], own_bias[1:2, :]
        else:
            small, absolute = refs[-2:]
            blocks = [(weights[index], start) for index, start, _ in all_spans]
            read_small(blocks, block, model // len(blocks), places_ref, small, absolute)
            at = pl.multiple_of(places_ref[len(blocks)] * width, 128)
            query_bias = absolute[6:7, pl.ds(at, width)]
            value_bias = absolute[6:7, pl.ds(at + 2 * width, width)]
        normed[...] = (normal_ref[...] * small[0:1, :] + small[1:2, :]).astype(BF16)
        packed = times_pieces(normed, weights, spans, slice(0, 3 * width))
        query[...] = (packed[:, :width] + query_bias).astype(BF16)
        key[...] = packed[:, width : 2 * width].astype(BF16)
        value[...] = (packed[:, 2 * width :] + value_bias).astype(BF16)
        valid = mask_ref[...]
        parts = []
        for head in range(width // HD):
            at = slice(head * HD, (head + 1) * HD)
            prob = probabilities(query[:, at], key[:, at], valid)
            parts.append(jnp.dot(prob.astype(BF16), value[:, at], preferred_element_type=F32))
        context[...] = jnp.concatenate(parts, axis=1).astype(BF16)
        times_pieces_back(context, weights, spans, slice(3 * width, 4 * width), own, other)

    in_vmem = pl.BlockSpec(memory_space=pltpu.VMEM)
    small_shape = [] if given else [shape_of(16, model, F32)] * 2
    out_shape = (
        [shape_of(slots, width, BF16)] * 4
        + [shape_of(half, model, F32), shape_of(half, model, BF16), shape_of(slots, model, BF16)]
        + small_shape
    )
    return pl.pallas_call(
        kernel,
        name="attention",
        in_specs=[pl.BlockSpec(memory_space=pltpu.SMEM)]
        + [in_vmem] * (2 + len(pieces) + len(given)),
        out_specs=[in_vmem] * len(out_shape),
        out_shape=out_shape,
        cost_estimate=low_cost(),
    )(places, normal, mask, *pieces, *given)


def attention_back(grad_att, context, mask, query, key, value, pieces, block, pitch):
    slots, width = context.shape
    model = grad_att[0].shape[1]
    half = slots // 2
    scale = HD ** (-0.5)
    spans = merged(spans_of(pieces, block, pitch), block, pitch)

    def kernel(grad_own, grad_other, context_ref, mask_ref, query_ref, key_ref, value_ref, *refs):
        weights = refs[: len(pieces)]
        packed, own, other, bias_sum = refs[len(pieces) :]
        grad_ref = stacked((grad_own, grad_other))
        valid = mask_ref[...]
        grad_context = times_pieces(
            grad_ref, weights, spans, slice(3 * width, 4 * width)
        ).astype(BF16)
        queries, keys, values = [], [], []
        for head in range(width // HD):
            at = slice(head * HD, (head + 1) * HD)
            q, k, v, g = query_ref[:, at], key_ref[:, at], value_ref[:, at], grad_context[:, at]
            prob = probabilities(q, k, valid)
            grad_prob = contract(g, v, 1, 1)
            dots = jnp.sum(prob * grad_prob, axis=-1, keepdims=True)
            grad_scores = (prob * (grad_prob - dots)).astype(BF16)
            queries.append(jnp.dot(grad_scores, k, preferred_element_type=F32) * scale)
            keys.append(contract(grad_scores, q, 0, 0) * scale)
            values.append(contract(prob.astype(BF16), g, 0, 0))
        for kind, parts in enumerate((queries, keys, values)):
            joined = jnp.concatenate(parts, axis=1).astype(BF16)
            packed[:, kind * width : (kind + 1) * width] = joined
            if kind != 1:
                at = (kind // 2) * width
                bias_sum[:, at : at + width] = jnp.sum(joined.astype(F32), axis=0, keepdims=True)
        packed[:, 3 * width :] = context_ref[...]
        grads = packed.at[:, : 3 * width]
        times_pieces_back(grads, weights, spans, slice(0, 3 * width), own, other)

    return pl.pallas_call(
        kernel,
        name="attention_back",
        out_shape=[
            shape_of(slots, 4 * width, BF16),
            shape_of(half, model, F32),
            shape_of(half, model, BF16),
            shape_of(1, 2 * width, F32),
        ],
        cost_estimate=low_cost(),
    )(*grad_att, context, mask, query, key, value, *pieces)


def hidden_layer(own, other, normed, bias, pieces, block):
    half, model = own.shape
    slots, hidden = 2 * half, bias.shape[1]
    spans = merged(spans_of(pieces, block, block), block, block)

    def kernel(own_ref, other_ref, normed_ref, bias_ref, *refs):
        message, slope = refs[len(pieces) :]
        left = stacked((own_ref, other_ref))
        pre_act = times_pieces(left, refs[: len(pieces)], spans, slice(0, hidden))
        pre_act = pre_act + bias_ref[...]
        cumulative = 0.5 * (1.0 + lax.erf(pre_act * ROOT_HALF))
        message[:slots, :] = (pre_act * cumulative).astype(BF16)
        message[slots:, : model // 2] = normed_ref[:half, model // 2 :]
        message[slots:, model // 2 :] = own_ref[:, model // 2 :]
        slope[...] = cumulative + pre_act * (
            INV_ROOT_TWO_PI * jnp.exp(-0.5 * pre_act * pre_act)
        )

    return pl.pallas_call(
        kernel,
        name="hidden_layer",
        out_shape=[shape_of(slots + half, hidden, BF16), shape_of(slots, hidden, F32)],
        cost_estimate=low_cost(),
    )(own, other, normed, bias, *pieces)


def hidden_back(grads, slope, up_pieces, down_pieces, block):
    model = grads[0].shape[1]
    slots, hidden = slope.shape
    half = slots // 2
    spans = merged(spans_of(up_pieces, block, block), block, block)
    down_spans = merged(spans_of(down_pieces, block, block), block, block)
    count = len(up_pieces)
    total = count + len(down_pieces)

    def kernel(grad_own, grad_other, slope_ref, *refs):
        grad_ref = stacked((grad_own, grad_other))
        up, down = refs[:count], refs[count:total]
        grad_pre, own, other, bias_sum = refs[total:]
        grad_active = times_pieces(grad_ref, down, down_spans, slice(0, hidden))
        low = (grad_active * slope_ref[...]).astype(BF16)
        grad_pre[...] = low
        bias_sum[...] = jnp.sum(low.astype(F32), axis=0, keepdims=True)
        times_pieces_back(grad_pre, up, spans, slice(0, hidden), own, other)

    return pl.pallas_call(
        kernel,
        name="hidden_back",
        out_shape=[
            shape_of(slots, hidden, BF16),
            shape_of(half, model, F32),
            shape_of(half, model, BF16),
            shape_of(1, hidden, F32),
        ],
        cost_estimate=low_cost(),
    )(*grads, slope, *up_pieces, *down_pieces)


def project_back(values, slots, pieces, block):
    columns = values.shape[1]
    spans = merged(spans_of(pieces, block, block), block, block)
    half = slots // 2

    def kernel(values_ref, *refs):
        left = values_ref.at[:slots, :]
        times_pieces_back(left, refs[: len(pieces)], spans, slice(0, columns), refs[-2], refs[-1])

    return pl.pallas_call(
        kernel,
        name="project_back",
        out_shape=[shape_of(half, D, F32), shape_of(half, D, BF16)],
        cost_estimate=low_cost(),
    )(values, *pieces)


def weight_grad(groups, rights, parts):
    columns = rights[0][0].shape[1]
    cut = D // 4
    arrays, index_of = [], {}

    def index(array):
        if id(array) not in index_of:
            index_of[id(array)] = len(arrays)
            arrays.append(array)
        return index_of[id(array)]

    right_rows = [(index(array), row, count) for array, row, count in rights]
    left_rows = [
        ([(index(array), row, count, column) for array, row, count, column in lefts], lo, hi)
        for lefts, lo, hi in groups
    ]
    size = cut // parts

    def kernel(*refs):
        outs = refs[len(arrays) :]
        targets = [(outs[part], cut + part * size) for part in range(parts)] + [(outs[-1], 0)]
        for lefts, lo, hi in left_rows:
            right = jnp.concatenate(
                [refs[at][row : row + count, lo:hi] for at, row, count in right_rows], axis=0
            )
            for target, first in targets:
                left = jnp.concatenate(
                    [
                        refs[at][row : row + count, column + first : column + first + target.shape[0]]
                        for at, row, count, column in lefts
                    ],
                    axis=0,
                )
                target[:, lo:hi] = contract(left, right, 0, 0).astype(target.dtype)

    return pl.pallas_call(
        kernel,
        name="weight_grad",
        out_shape=[shape_of(size, columns, BF16)] * parts + [shape_of(cut, columns, F32)],
        cost_estimate=low_cost(),
    )(*arrays)


def norm_of(values):
    mean = jnp.mean(values, axis=-1, keepdims=True)
    centered = values - mean
    scale = lax.rsqrt(jnp.mean(centered * centered, axis=-1, keepdims=True) + EPSILON)
    return centered * scale, scale


def valid_rows(rows, places_ref):
    slot = lax.broadcasted_iota(jnp.int32, (rows, 1), 0) + places_ref[places_ref.shape[0] - 2]
    return (slot < places_ref[places_ref.shape[0] - 1]).astype(F32)


def norm_grad(normal, scale, gain, grad):
    weighted = grad * gain
    return scale * (
        weighted
        - jnp.mean(weighted, axis=-1, keepdims=True)
        - normal * jnp.mean(weighted * normal, axis=-1, keepdims=True)
    )


def column_sum(values):
    return jnp.sum(values, axis=0, keepdims=True)


def second_norm_back(middle, gain, low, other_low, grad_res):
    rows, model = middle.shape

    def kernel(middle_ref, gain_ref, low_ref, other_ref, res_ref, *outs):
        grad_middle, grad_att, sums = outs
        grad = low_ref[...].astype(F32) + other_ref[...].astype(F32)
        res = res_ref[...].astype(F32)
        n, scale = norm_of(middle_ref[...])
        total = res + norm_grad(n, scale, gain_ref[...], grad)
        grad_middle[...] = total
        rounded = total.astype(BF16)
        grad_att[...] = rounded
        sums[0:1, :] = column_sum(rounded.astype(F32))
        sums[1:2, :] = column_sum(grad * n)
        sums[2:3, :] = column_sum(grad)
        sums[3:4, :] = column_sum(res)

    return pl.pallas_call(
        kernel,
        name="second_norm_back",
        out_shape=[
            shape_of(rows, model, F32),
            shape_of(rows, model, BF16),
            shape_of(4, model, F32),
        ],
        cost_estimate=low_cost(),
    )(middle, gain, low, other_low, grad_res)


def place_blocks(target, rows, values, places_ref):
    count = places_ref.shape[0] - 3
    width = values.shape[1] // count
    if width % 128:
        target[rows, :] = values
        return
    for block in range(count):
        to = pl.ds(pl.multiple_of(places_ref[block] * width, 128), width)
        target[rows, to] = values[:, block * width : (block + 1) * width]


def finish(middle, entering, attended, low, other_low, bias, places):
    rows, model = middle.shape

    def kernel(
        places_ref, middle_ref, entering_ref, attended_ref, low_ref, other_ref, bias_ref,
        output, stats
    ):
        branch = low_ref[...].astype(F32) + other_ref[...].astype(F32) + bias_ref[...]
        result = middle_ref[...] + branch
        place_blocks(output, slice(None), result.astype(BF16), places_ref)
        good = valid_rows(rows, places_ref)
        lane = lax.broadcasted_iota(jnp.int32, (1, 128), 1)
        row = jnp.where(lane == 5, column_sum(good), 0.0)
        terms = (entering_ref[...], attended_ref[...], middle_ref[...], branch, result)
        for index, term in enumerate(terms):
            total = jnp.sum(column_sum(term * term * good), axis=1, keepdims=True)
            row = jnp.where(lane == index, total, row)
        stats[...] = row

    in_vmem = pl.BlockSpec(memory_space=pltpu.VMEM)
    return pl.pallas_call(
        kernel,
        name="finish",
        in_specs=[pl.BlockSpec(memory_space=pltpu.SMEM)] + [in_vmem] * 6,
        out_specs=[in_vmem] * 2,
        out_shape=[shape_of(rows, model, BF16), shape_of(1, 128, F32)],
        cost_estimate=low_cost(),
    )(places, middle, entering, attended, low, other_low, bias)


def first_norm_back(
    inputs, gain, low, other_low, grad_middle, sums, up_sum, qv_sum, stats, places
):
    rows, model = inputs.shape

    def kernel(
        places_ref, inputs_ref, gain_ref, low_ref, other_ref, middle_ref,
        sums_ref, up_ref, qv_ref, stats_ref, grad_inputs, message
    ):
        grad = low_ref[...].astype(F32) + other_ref[...].astype(F32)
        valid = valid_rows(rows, places_ref)
        n, scale = norm_of(inputs_ref[...].astype(F32) * valid)
        total = middle_ref[...] + norm_grad(n, scale, gain_ref[...], grad)
        total = total * valid
        vectors = jnp.concatenate(
            [column_sum(grad * n), column_sum(grad), sums_ref[...]], axis=0
        )
        message[6:7, :] = up_ref[...]
        message[7:8, :] = jnp.zeros((1, model), F32)
        message[7:8, : qv_ref.shape[1]] = qv_ref[...]
        message[7:8, model - 128 :] = stats_ref[...]
        place_blocks(grad_inputs, slice(None), total, places_ref)
        place_blocks(message, slice(0, 6), vectors, places_ref)

    in_vmem = pl.BlockSpec(memory_space=pltpu.VMEM)
    return pl.pallas_call(
        kernel,
        name="first_norm_back",
        in_specs=[pl.BlockSpec(memory_space=pltpu.SMEM)] + [in_vmem] * 9,
        out_specs=[in_vmem] * 2,
        out_shape=[shape_of(rows, model, F32), shape_of(8, model, F32)],
        cost_estimate=low_cost(),
    )(
        places, inputs, gain, low, other_low, grad_middle, sums, up_sum, qv_sum, stats
    )


def halves_low(own, other):
    low = round_low(own + swap(other, "ctx").astype(F32))
    return low, swap(low, "tp")


def halves_sum(own, other):
    low = round_low(own + swap(other, "ctx").astype(F32))
    return low.astype(F32) + swap(low, "tp").astype(F32)


def coded(values):
    high = lax.reduce_precision(values, 8, 7)
    return rows_of(high.astype(BF16), round_low(values - high))


def decoded(rows):
    return lower(rows).astype(F32) + upper(rows).astype(F32)


def with_other(own):
    return jnp.concatenate([own, swap(own, "ctx")], axis=0)


def body(
    inputs,
    lengths,
    grad_out,
    ln1_gain,
    ln1_shift,
    w_qkv,
    b_qv,
    w_proj,
    b_proj,
    ln2_gain,
    ln2_shift,
    w_up,
    b_up,
    w_down,
    b_down,
):
    n = lax.axis_size("fsdp")
    cube = is_cube()
    core = lax.axis_index("ctx")
    place = lax.axis_index("fsdp")
    rows = w_up.shape[0]
    head_cols = w_proj.shape[1] // 2
    hidden = w_up.shape[1] // 2
    own_slots = inputs.shape[1]
    width = D // n

    qkv_halves = w_qkv.reshape(rows, 3, 2, head_cols)
    proj_halves = w_proj.reshape(rows, 2, head_cols)
    up_halves = w_up.reshape(rows, 2, hidden)
    down_halves = w_down.reshape(rows, 2, hidden)

    def first_half(which):
        return jnp.concatenate(
            [
                lax.dynamic_index_in_dim(qkv_halves, which, 2, keepdims=False).reshape(
                    rows, 3 * head_cols
                ),
                lax.dynamic_index_in_dim(proj_halves, which, 1, keepdims=False),
            ],
            axis=1,
        )

    def half_of(halves, which):
        return lax.dynamic_index_in_dim(halves, which, 1, keepdims=False)

    def by_core(own, other, axis):
        return jnp.where(
            core == 0,
            jnp.concatenate([own, other], axis=axis),
            jnp.concatenate([other, own], axis=axis),
        )

    small = jnp.concatenate(
        [
            jnp.stack([ln1_gain, ln1_shift, b_proj, ln2_gain, ln2_shift, b_down, b_qv[:, 0]]),
            b_up.reshape(2, rows),
        ]
    )
    small_both = by_core(small, swap(small, "ctx"), 1)
    first_own, first_other = first_half(core), first_half(1 - core)
    first_mine = by_core(first_own, swap(first_other, "ctx"), 0)
    small_flat = jnp.zeros((16 * 2 * rows,), BF16)
    small_flat = small_flat.at[: 9 * 2 * rows].set(small_both.reshape(-1))
    cols = first_mine.shape[1]
    small_rows = -(-16 * 2 * rows // cols)
    small_rows_padded = -(-small_rows // 8) * 8
    small_block = jnp.zeros((small_rows_padded * cols,), BF16)
    small_block = small_block.at[: 16 * 2 * rows].set(small_flat).reshape(small_rows_padded, cols)

    first_shard = jnp.concatenate([first_mine, small_block], axis=0)
    first_shard, inputs, grad_out, up_halves, down_halves = tie(
        first_shard, inputs, grad_out, up_halves, down_halves
    )
    u, d = (
        by_core(half_of(t, core), swap(half_of(t, 1 - core), "ctx"), 0)
        for t in (up_halves, down_halves)
    )
    absolute, relative = absolute_places(), relative_blocks()

    def to_relative(array):
        blocks = array.reshape(array.shape[0], n, width)
        return jnp.take(blocks, absolute, axis=1).reshape(array.shape)

    grad_own = to_relative(grad_out[0])
    length = lengths[0]
    own_ids = core * own_slots + jnp.arange(own_slots, dtype=jnp.int32)
    other_ids = (1 - core) * own_slots + jnp.arange(own_slots, dtype=jnp.int32)
    slot_ids = jnp.concatenate([own_ids, other_ids])
    key_valid = slot_ids < length
    row_valid = key_valid.astype(F32)[:, None]
    places = jnp.concatenate([absolute, jnp.stack([core, core * own_slots, length])])

    inputs_own = to_relative(inputs[0])
    entering_all = with_other(inputs_own).astype(F32) * row_valid
    grads = (grad_own, swap(grad_own, "ctx"))
    normal_one, _ = norm_of(entering_all)
    slots = 2 * own_slots
    f = first_shard
    if cube:
        f_far, f_x = flip(f, FAR_BIT), flip(f, X_BIT)
        grad_far = flip(grad_own[:, D // 2 :], X_BIT)
        f_far, f_x, grad_far, u, d = tie(f_far, f_x, grad_far, u, d)
        u_x = flip(u, X_BIT)
        f_near = flip(rows_of(f, f_far), NEAR_BIT)
        u_far, f_far_x, d_x = flip(u, FAR_BIT), flip(f_far, X_BIT), flip(d, X_BIT)
        f_near, u_far, f_far_x, u_x, d_x, u, d = tie(f_near, u_far, f_far_x, u_x, d_x, u, d)
        u_near = flip(rows_of(u, u_far), NEAR_BIT)
        d_far, f_near_x, u_far_x = flip(d, FAR_BIT), flip(f_near, X_BIT), flip(u_far, X_BIT)
        d_far, f_near_x, u_far_x, u_near, d, normal_one = tie(
            d_far, f_near_x, u_far_x, u_near, d, normal_one
        )
        d_near = flip(rows_of(d, d_far), NEAR_BIT)
        u_near_x = flip(u_near, X_BIT)
        first_pieces = [f, f_far, f_near, f_x, f_far_x, f_near_x]
    else:
        first_pieces, up_pieces, down_pieces = (
            [lax.all_gather(t, "fsdp", tiled=True)] for t in (f, u, d)
        )
    block, pitch = 2 * rows, 2 * rows + small_rows_padded
    vectors = qv_bias = None
    if not cube:
        whole = first_pieces[0].reshape(n, pitch, cols)
        first_pieces, pitch = [whole[:, :block].reshape(D, cols)], block
        small_abs = whole[:, block:].reshape(n, -1)[:, : 16 * 2 * rows]
        small_abs = small_abs.reshape(n, 16, 2 * rows).astype(F32)
        vectors = small_abs.transpose(1, 0, 2).reshape(16, D)
        qv_all = small_abs[:, 6].reshape(2, 2, head_cols)
        qv_bias = lax.dynamic_index_in_dim(qv_all, core, 1, keepdims=False)

    key_mask = row_valid.reshape(1, slots)
    query, key, value, context, att_own, att_other, normed, *found = attention(
        normal_one, vectors, qv_bias, key_mask, first_pieces, block, pitch, places
    )
    if cube:
        vectors, vectors_abs = found
        small_abs = vectors_abs.reshape(16, n, 2 * rows).transpose(1, 0, 2)
    gain_one, _, proj_bias, gain_two, shift_two, down_bias = (vectors[i] for i in range(6))
    up_all = small_abs[:, 7:9].reshape(n, 2, 2, rows).transpose(0, 2, 1, 3).reshape(2, hidden)
    up_bias = lax.dynamic_index_in_dim(up_all, core, 0, keepdims=False)
    if cube:
        d_near, u_near_x, d_far, att_own, att_other = tie(
            d_near, u_near_x, d_far, att_own, att_other
        )
        d_rest_x = flip(rows_of(d_far, d_near), X_BIT)
        up_pieces = [u, u_far, u_near, u_x, u_far_x, u_near_x]
    att_low, att_tp = halves_low(att_own, att_other)
    attended = att_low.astype(F32) + att_tp.astype(F32) + proj_bias
    entering = entering_all[:own_slots]
    middle = entering + attended
    normal_two, _ = norm_of(middle)
    normed_two_own = (normal_two * gain_two + shift_two).astype(BF16)
    normed_two_other = swap(normed_two_own, "ctx")
    active, slope = hidden_layer(
        normed_two_own, normed_two_other, normed, up_bias[None], up_pieces, block
    )
    if cube:
        active, slope, d_rest_x = tie(active, slope, d_rest_x)
        active_far = flip(active, X_BIT)
        down_pieces = [d, d_far, d_near, d_x, d_rest_x]
    grad_pre, gn_own, gn_other, sum_up_bias = hidden_back(
        grads, slope, up_pieces, down_pieces, block
    )
    gn_low = round_low(gn_own + swap(gn_other, "ctx").astype(F32))
    if cube:
        gn_low, active = tie(gn_low, active)
    gn_tp = swap(gn_low, "tp")
    branch_own, branch_other = project_back(active, slots, down_pieces, block)
    if cube:
        gn_low, gn_tp, active_far, grad_pre, branch_own, branch_other = tie(
            gn_low, gn_tp, active_far, grad_pre, branch_own, branch_other
        )
        pre_far = flip(grad_pre, X_BIT)
        size, half = own_slots, D // 2
    grad_middle, grad_att_own, sums = second_norm_back(
        middle, gain_two[None], gn_low, gn_tp, grad_own
    )
    if cube:
        grad_att_own, active_far, branch_own, branch_other = tie(
            grad_att_own, active_far, branch_own, branch_other
        )
        att_far = flip(grad_att_own[:, half:], X_BIT)
        down_high, down_two = weight_grad(
            [
                (
                    [(t, 0, size, 0) for t in (*grads, grad_far, swap(grad_far, "ctx"))],
                    0,
                    hidden,
                )
            ],
            [(active, 0, slots), (active_far, 0, slots)],
            1,
        )
    grad_att_other = swap(grad_att_own, "ctx")
    if cube:
        down_high, grad_att_other = tie(down_high, grad_att_other)
        down_near = flip(down_high, NEAR_BIT)
    branch_low, branch_tp = halves_low(branch_own, branch_other)
    packed, gn_one_own, gn_one_other, sum_qv_bias = attention_back(
        (grad_att_own, grad_att_other), context, key_mask, query, key, value, first_pieces, block, pitch
    )
    if cube:
        pre_far, att_far, down_near, packed, gn_one_own, gn_one_other, branch_low, branch_tp = tie(
            pre_far, att_far, down_near, packed, gn_one_own, gn_one_other, branch_low, branch_tp
        )
        packed_far = flip(packed, X_BIT)
        down_far = flip(round_low(upper(down_two) + upper(down_near).astype(F32)), FAR_BIT)
        normed_swapped = swap(active_far[slots:], "ctx")
        up_high, up_two = weight_grad(
            [
                (
                    [
                        (normed_two_own, 0, size, 0),
                        (normed_two_other, 0, size, 0),
                        (active_far, slots, size, half),
                        (normed_swapped, 0, size, half),
                    ],
                    0,
                    hidden,
                )
            ],
            [(grad_pre, 0, slots), (pre_far, 0, slots)],
            1,
        )
    gn_one_low = round_low(gn_one_own + swap(gn_one_other, "ctx").astype(F32))
    if cube:
        gn_one_low, down_far = tie(gn_one_low, down_far)
    gn_one_tp = swap(gn_one_low, "tp")
    if cube:
        att_swapped = swap(att_far, "ctx")
        up_near = flip(up_high, NEAR_BIT)
        *first_high, first_two = weight_grad(
            [
                (
                    [
                        (normed, 0, slots, 0),
                        (active_far, slots, size, 0),
                        (normed_swapped, 0, size, 0),
                    ],
                    0,
                    3 * head_cols,
                ),
                (
                    [
                        (t, 0, size, 0)
                        for t in (grad_att_own, grad_att_other, att_far, att_swapped)
                    ],
                    3 * head_cols,
                    4 * head_cols,
                ),
            ],
            [(packed, 0, slots), (packed_far, 0, slots)],
            2,
        )
        first_high, gn_one_low, gn_one_tp, up_near = tie(
            first_high, gn_one_low, gn_one_tp, up_near
        )
        up_far = flip(round_low(upper(up_two) + upper(up_near).astype(F32)), FAR_BIT)
    else:
        sum_down = scatter_sum(contract(rows_of(*grads), active[:slots], 0, 0))
        sum_up = scatter_sum(contract(rows_of(normed_two_own, normed_two_other), grad_pre, 0, 0))
        sum_first = jnp.concatenate(
            [
                scatter_sum(contract(normed, packed[:, : 3 * head_cols], 0, 0)),
                scatter_sum(
                    contract(rows_of(grad_att_own, grad_att_other), context, 0, 0)
                ),
            ],
            axis=1,
        )
    output, stats = finish(
        middle, entering, attended, branch_low, branch_tp, down_bias[None], places
    )
    output = output[None]
    grad_inputs, message = first_norm_back(
        inputs_own,
        gain_one[None],
        gn_one_low,
        gn_one_tp,
        grad_middle,
        sums,
        sum_up_bias,
        sum_qv_bias,
        stats,
        places,
    )
    grad_inputs = grad_inputs[None]

    if cube:
        message = message + flip(message, X_BIT)
        first_near = [flip(rows_of(first_high[1], coded(message)), NEAR_BIT)]
        first_near[0], first_high, up_far = tie(first_near[0], first_high, up_far)
        message = message + decoded(first_near[0][block:])
        first_low = round_low(upper(first_two) + first_near[0][:block].astype(F32))
        far_rows, first_rest = tie(rows_of(first_low, coded(message)), first_high[0])
        first_far = flip(far_rows, FAR_BIT)
        first_near.append(flip(first_rest, NEAR_BIT))
        first_near[1], up_far = tie(first_near[1], up_far)
        sum_first = (
            lower(first_two) + first_near[1].astype(F32) + first_far[:block].astype(F32)
        )
        sum_down = lower(down_two) + lower(down_near).astype(F32) + down_far.astype(F32)
        sum_up = lower(up_two) + lower(up_near).astype(F32) + up_far.astype(F32)
        message = message + decoded(first_far[block:])
    else:
        message = lax.psum(message, "fsdp")
    other_message = swap(message, "ctx")
    at = 2 * place + core
    vector_own = lax.dynamic_slice_in_dim(
        message[:6] + other_message[:6], at * rows, rows, 1
    )
    totals = (message[7] + other_message[7])[D - 128 : D - 122]
    rms = jnp.sqrt(totals[:5] / (totals[5] * D))
    qv_sum = by_core(
        message[7, : 2 * head_cols].reshape(2, 1, head_cols),
        other_message[7, : 2 * head_cols].reshape(2, 1, head_cols),
        1,
    ).reshape(-1)
    qv_mine = lax.dynamic_slice_in_dim(qv_sum, at * rows, rows, 0)
    up_sum = by_core(message[6], other_message[6], 0)
    up_mine = lax.dynamic_slice_in_dim(up_sum, at * 2 * rows, 2 * rows, 0)

    def owned(total):
        mine = lax.dynamic_slice_in_dim(total, core * rows, rows, 0)
        theirs = swap(lax.dynamic_slice_in_dim(total, (1 - core) * rows, rows, 0), "ctx")
        return mine, theirs

    mine, theirs = owned(sum_first)
    parts = [
        by_core(mine[:, at : at + head_cols], theirs[:, at : at + head_cols], 1)
        for at in range(0, 4 * head_cols, head_cols)
    ]
    grad_w_qkv, grad_w_proj = jnp.stack(parts[:3], axis=1), parts[3]
    grad_w_up = by_core(*owned(sum_up), 1)
    grad_w_down = by_core(*owned(sum_down), 1)
    return (
        output,
        grad_inputs,
        vector_own[0],
        vector_own[1],
        grad_w_qkv,
        qv_mine[:, None],
        grad_w_proj,
        vector_own[2],
        vector_own[3],
        vector_own[4],
        grad_w_up,
        up_mine[:, None],
        grad_w_down,
        vector_own[5],
        rms,
    )


def solution(mesh):
    both = ("fsdp", "ctx")
    rows, vector, matrix = P("fsdp", "ctx", None), P(both), P(both, "tp")
    in_specs = (
        rows,
        P("fsdp"),
        rows,
        vector,
        vector,
        P(both, None, "tp"),
        matrix,
        matrix,
        vector,
        vector,
        vector,
        matrix,
        matrix,
        matrix,
        vector,
    )
    out_specs = (
        rows,
        rows,
        vector,
        vector,
        P(both, None, "tp"),
        matrix,
        matrix,
        vector,
        vector,
        vector,
        matrix,
        matrix,
        matrix,
        vector,
        P(),
    )
    return jax.shard_map(body, mesh=mesh, in_specs=in_specs, out_specs=out_specs, check_vma=False)
```

```python
import jax
import jax.numpy as jnp
from jax import lax
from jax.experimental import pallas as pl
from jax.experimental.pallas import tpu as pltpu
from jax.sharding import PartitionSpec as P

D = 1024
HD = 64
EPSILON = 1e-06
MASK_FILL = -1e30
ROOT_HALF = 0.7071067811865476
INV_ROOT_TWO_PI = 0.3989422804014327
F32 = jnp.float32
BF16 = jnp.bfloat16


def contract(left, right, left_dim, right_dim):
    return lax.dot_general(
        left, right, (((left_dim,), (right_dim,)), ((), ())), preferred_element_type=F32
    )


def round_low(values):
    return lax.reduce_precision(values, 8, 7).astype(BF16)


def swap(array, axis):
    return lax.ppermute(array, axis, [(0, 1), (1, 0)])


def flip(array, bit):
    n = lax.axis_size("fsdp")
    return lax.ppermute(array, "fsdp", [(i, i ^ bit) for i in range(n)])


X_BIT, NEAR_BIT, FAR_BIT = 1, 2, 4


def is_cube():
    return lax.axis_size("fsdp") == 8


def turned_bits(blocks):
    return (blocks % 2) * 4 + (blocks // 2 % 2) * 2 + blocks // 4


def relative_blocks():
    spots = jnp.arange(lax.axis_size("fsdp"), dtype=jnp.int32)
    if not is_cube():
        return spots
    return turned_bits(spots ^ lax.axis_index("fsdp"))


def absolute_places():
    blocks = jnp.arange(lax.axis_size("fsdp"), dtype=jnp.int32)
    if not is_cube():
        return blocks
    return turned_bits(blocks) ^ lax.axis_index("fsdp")


def tie(*values):
    return lax.optimization_barrier(values)


def rows_of(*pieces):
    return jnp.concatenate(pieces, axis=0)


def upper(array):
    return array[array.shape[0] // 2 :]


def lower(array):
    return array[: array.shape[0] // 2]


def scatter_sum(partial):
    low = round_low(partial)
    return lax.psum_scatter(low, "fsdp", scatter_dimension=0, tiled=True).astype(F32)


def low_cost():
    return pl.CostEstimate(flops=1000, transcendentals=0, bytes_accessed=1000)


def probabilities(query, key, mask):
    scores = contract(query, key, 1, 1) * (HD ** (-0.5))
    scores = jnp.where(mask > 0, scores, MASK_FILL)
    raised = jnp.exp(scores - jnp.max(scores, axis=-1, keepdims=True))
    return raised / jnp.sum(raised, axis=-1, keepdims=True)


def spans_of(pieces, block, pitch):
    spans, row = [], 0
    for index, piece in enumerate(pieces):
        for start in range(0, piece.shape[0], pitch):
            spans.append((index, start, row))
            row += block
    return spans


def merged(spans, block, pitch):
    if block != pitch:
        return [(index, start, row, block) for index, start, row in spans]
    joined = []
    for index, start, row in spans:
        if joined and joined[-1][0] == index:
            last = joined[-1]
            joined[-1] = (index, last[1], last[2], last[3] + block)
        else:
            joined.append((index, start, row, block))
    return joined


def times_pieces(left, pieces, spans, columns):
    total = None
    for index, start, row, size in spans:
        part = jnp.dot(
            left[:, row : row + size],
            pieces[index][start : start + size, columns],
            preferred_element_type=F32,
        )
        total = part if total is None else total + part
    return total


def times_pieces_back(left, pieces, spans, columns, own, other):
    half = own.shape[0]
    for index, start, row, size in spans:
        weight = pieces[index][start : start + size, columns]
        own[:, row : row + size] = contract(left[:half, :], weight, 1, 1)
        other[:, row : row + size] = contract(left[half:, :], weight, 1, 1).astype(BF16)


def shape_of(rows, columns, dtype):
    return jax.ShapeDtypeStruct((rows, columns), dtype)


def stacked(refs):
    return jnp.concatenate([ref[...] for ref in refs], axis=0)


def read_small(blocks, block, width, places_ref, relative, absolute):
    for index, (ref, start) in enumerate(blocks):
        lines = [
            ref[
                start + block + vector // 8 : start + block + vector // 8 + 1,
                vector % 8 * width : (vector % 8 + 1) * width,
            ]
            for vector in range(16)
        ]
        values = jnp.concatenate(lines, axis=0).astype(F32)
        relative[:, index * width : (index + 1) * width] = values
        to = pl.ds(pl.multiple_of(places_ref[index] * width, 128), width)
        absolute[:, to] = values


def attention(normal, vectors, bias, mask, pieces, block, pitch, places):
    slots, model = normal.shape
    width = pieces[0].shape[1] // 4
    half = slots // 2
    all_spans = spans_of(pieces, block, pitch)
    spans = merged(all_spans, block, pitch)
    given = [] if vectors is None else [vectors, bias]

    def kernel(places_ref, normal_ref, mask_ref, *refs):
        weights = refs[: len(pieces)]
        query, key, value, context, own, other, normed = refs[len(pieces) + len(given) :][:7]
        if given:
            small, own_bias = refs[len(pieces) : len(pieces) + 2]
            query_bias, value_bias = own_bias[0:1, :], own_bias[1:2, :]
        else:
            small, absolute = refs[-2:]
            blocks = [(weights[index], start) for index, start, _ in all_spans]
            read_small(blocks, block, model // len(blocks), places_ref, small, absolute)
            at = pl.multiple_of(places_ref[len(blocks)] * width, 128)
            query_bias = absolute[6:7, pl.ds(at, width)]
            value_bias = absolute[6:7, pl.ds(at + 2 * width, width)]
        normed[...] = (normal_ref[...] * small[0:1, :] + small[1:2, :]).astype(BF16)
        packed = times_pieces(normed, weights, spans, slice(0, 3 * width))
        query[...] = (packed[:, :width] + query_bias).astype(BF16)
        key[...] = packed[:, width : 2 * width].astype(BF16)
        value[...] = (packed[:, 2 * width :] + value_bias).astype(BF16)
        valid = mask_ref[...]
        parts = []
        for head in range(width // HD):
            at = slice(head * HD, (head + 1) * HD)
            prob = probabilities(query[:, at], key[:, at], valid)
            parts.append(jnp.dot(prob.astype(BF16), value[:, at], preferred_element_type=F32))
        context[...] = jnp.concatenate(parts, axis=1).astype(BF16)
        times_pieces_back(context, weights, spans, slice(3 * width, 4 * width), own, other)

    in_vmem = pl.BlockSpec(memory_space=pltpu.VMEM)
    small_shape = [] if given else [shape_of(16, model, F32)] * 2
    out_shape = (
        [shape_of(slots, width, BF16)] * 4
        + [shape_of(half, model, F32), shape_of(half, model, BF16), shape_of(slots, model, BF16)]
        + small_shape
    )
    return pl.pallas_call(
        kernel,
        name="attention",
        in_specs=[pl.BlockSpec(memory_space=pltpu.SMEM)]
        + [in_vmem] * (2 + len(pieces) + len(given)),
        out_specs=[in_vmem] * len(out_shape),
        out_shape=out_shape,
        cost_estimate=low_cost(),
    )(places, normal, mask, *pieces, *given)


def attention_back(grad_att, context, mask, query, key, value, pieces, block, pitch):
    slots, width = context.shape
    model = grad_att[0].shape[1]
    half = slots // 2
    scale = HD ** (-0.5)
    spans = merged(spans_of(pieces, block, pitch), block, pitch)

    def kernel(grad_own, grad_other, context_ref, mask_ref, query_ref, key_ref, value_ref, *refs):
        weights = refs[: len(pieces)]
        packed, own, other, bias_sum = refs[len(pieces) :]
        grad_ref = stacked((grad_own, grad_other))
        valid = mask_ref[...]
        grad_context = times_pieces(
            grad_ref, weights, spans, slice(3 * width, 4 * width)
        ).astype(BF16)
        queries, keys, values = [], [], []
        for head in range(width // HD):
            at = slice(head * HD, (head + 1) * HD)
            q, k, v, g = query_ref[:, at], key_ref[:, at], value_ref[:, at], grad_context[:, at]
            prob = probabilities(q, k, valid)
            grad_prob = contract(g, v, 1, 1)
            dots = jnp.sum(prob * grad_prob, axis=-1, keepdims=True)
            grad_scores = (prob * (grad_prob - dots)).astype(BF16)
            queries.append(jnp.dot(grad_scores, k, preferred_element_type=F32) * scale)
            keys.append(contract(grad_scores, q, 0, 0) * scale)
            values.append(contract(prob.astype(BF16), g, 0, 0))
        for kind, parts in enumerate((queries, keys, values)):
            joined = jnp.concatenate(parts, axis=1).astype(BF16)
            packed[:, kind * width : (kind + 1) * width] = joined
            if kind != 1:
                at = (kind // 2) * width
                bias_sum[:, at : at + width] = jnp.sum(joined.astype(F32), axis=0, keepdims=True)
        packed[:, 3 * width :] = context_ref[...]
        grads = packed.at[:, : 3 * width]
        times_pieces_back(grads, weights, spans, slice(0, 3 * width), own, other)

    return pl.pallas_call(
        kernel,
        name="attention_back",
        out_shape=[
            shape_of(slots, 4 * width, BF16),
            shape_of(half, model, F32),
            shape_of(half, model, BF16),
            shape_of(1, 2 * width, F32),
        ],
        cost_estimate=low_cost(),
    )(*grad_att, context, mask, query, key, value, *pieces)


def hidden_layer(own, other, normed, bias, pieces, block):
    half, model = own.shape
    slots, hidden = 2 * half, bias.shape[1]
    spans = merged(spans_of(pieces, block, block), block, block)

    def kernel(own_ref, other_ref, normed_ref, bias_ref, *refs):
        message, slope = refs[len(pieces) :]
        left = stacked((own_ref, other_ref))
        pre_act = times_pieces(left, refs[: len(pieces)], spans, slice(0, hidden))
        pre_act = pre_act + bias_ref[...]
        cumulative = 0.5 * (1.0 + lax.erf(pre_act * ROOT_HALF))
        message[:slots, :] = (pre_act * cumulative).astype(BF16)
        message[slots:, : model // 2] = normed_ref[:half, model // 2 :]
        message[slots:, model // 2 :] = own_ref[:, model // 2 :]
        slope[...] = cumulative + pre_act * (
            INV_ROOT_TWO_PI * jnp.exp(-0.5 * pre_act * pre_act)
        )

    return pl.pallas_call(
        kernel,
        name="hidden_layer",
        out_shape=[shape_of(slots + half, hidden, BF16), shape_of(slots, hidden, F32)],
        cost_estimate=low_cost(),
    )(own, other, normed, bias, *pieces)


def hidden_back(grads, slope, up_pieces, down_pieces, block):
    model = grads[0].shape[1]
    slots, hidden = slope.shape
    half = slots // 2
    spans = merged(spans_of(up_pieces, block, block), block, block)
    down_spans = merged(spans_of(down_pieces, block, block), block, block)
    count = len(up_pieces)
    total = count + len(down_pieces)

    def kernel(grad_own, grad_other, slope_ref, *refs):
        grad_ref = stacked((grad_own, grad_other))
        up, down = refs[:count], refs[count:total]
        grad_pre, own, other, bias_sum = refs[total:]
        grad_active = times_pieces(grad_ref, down, down_spans, slice(0, hidden))
        low = (grad_active * slope_ref[...]).astype(BF16)
        grad_pre[...] = low
        bias_sum[...] = jnp.sum(low.astype(F32), axis=0, keepdims=True)
        times_pieces_back(grad_pre, up, spans, slice(0, hidden), own, other)

    return pl.pallas_call(
        kernel,
        name="hidden_back",
        out_shape=[
            shape_of(slots, hidden, BF16),
            shape_of(half, model, F32),
            shape_of(half, model, BF16),
            shape_of(1, hidden, F32),
        ],
        cost_estimate=low_cost(),
    )(*grads, slope, *up_pieces, *down_pieces)


def project_back(values, slots, pieces, block):
    columns = values.shape[1]
    spans = merged(spans_of(pieces, block, block), block, block)
    half = slots // 2

    def kernel(values_ref, *refs):
        left = values_ref.at[:slots, :]
        times_pieces_back(left, refs[: len(pieces)], spans, slice(0, columns), refs[-2], refs[-1])

    return pl.pallas_call(
        kernel,
        name="project_back",
        out_shape=[shape_of(half, D, F32), shape_of(half, D, BF16)],
        cost_estimate=low_cost(),
    )(values, *pieces)


def weight_grad(groups, rights, parts):
    columns = rights[0][0].shape[1]
    cut = D // 4
    arrays, index_of = [], {}

    def index(array):
        if id(array) not in index_of:
            index_of[id(array)] = len(arrays)
            arrays.append(array)
        return index_of[id(array)]

    right_rows = [(index(array), row, count) for array, row, count in rights]
    left_rows = [
        ([(index(array), row, count, column) for array, row, count, column in lefts], lo, hi)
        for lefts, lo, hi in groups
    ]
    size = cut // parts

    def kernel(*refs):
        outs = refs[len(arrays) :]
        targets = [(outs[part], cut + part * size) for part in range(parts)] + [(outs[-1], 0)]
        for lefts, lo, hi in left_rows:
            right = jnp.concatenate(
                [refs[at][row : row + count, lo:hi] for at, row, count in right_rows], axis=0
            )
            for target, first in targets:
                left = jnp.concatenate(
                    [
                        refs[at][row : row + count, column + first : column + first + target.shape[0]]
                        for at, row, count, column in lefts
                    ],
                    axis=0,
                )
                target[:, lo:hi] = contract(left, right, 0, 0).astype(target.dtype)

    return pl.pallas_call(
        kernel,
        name="weight_grad",
        out_shape=[shape_of(size, columns, BF16)] * parts + [shape_of(cut, columns, F32)],
        cost_estimate=low_cost(),
    )(*arrays)


def norm_of(values):
    mean = jnp.mean(values, axis=-1, keepdims=True)
    centered = values - mean
    scale = lax.rsqrt(jnp.mean(centered * centered, axis=-1, keepdims=True) + EPSILON)
    return centered * scale, scale


def valid_rows(rows, places_ref):
    slot = lax.broadcasted_iota(jnp.int32, (rows, 1), 0) + places_ref[places_ref.shape[0] - 2]
    return (slot < places_ref[places_ref.shape[0] - 1]).astype(F32)


def norm_grad(normal, scale, gain, grad):
    weighted = grad * gain
    return scale * (
        weighted
        - jnp.mean(weighted, axis=-1, keepdims=True)
        - normal * jnp.mean(weighted * normal, axis=-1, keepdims=True)
    )


def column_sum(values):
    return jnp.sum(values, axis=0, keepdims=True)


def second_norm_back(middle, gain, low, other_low, grad_res):
    rows, model = middle.shape

    def kernel(middle_ref, gain_ref, low_ref, other_ref, res_ref, *outs):
        grad_middle, grad_att, sums = outs
        grad = low_ref[...].astype(F32) + other_ref[...].astype(F32)
        res = res_ref[...].astype(F32)
        n, scale = norm_of(middle_ref[...])
        total = res + norm_grad(n, scale, gain_ref[...], grad)
        grad_middle[...] = total
        rounded = total.astype(BF16)
        grad_att[...] = rounded
        sums[0:1, :] = column_sum(rounded.astype(F32))
        sums[1:2, :] = column_sum(grad * n)
        sums[2:3, :] = column_sum(grad)
        sums[3:4, :] = column_sum(res)

    return pl.pallas_call(
        kernel,
        name="second_norm_back",
        out_shape=[
            shape_of(rows, model, F32),
            shape_of(rows, model, BF16),
            shape_of(4, model, F32),
        ],
        cost_estimate=low_cost(),
    )(middle, gain, low, other_low, grad_res)


def place_blocks(target, rows, values, places_ref):
    count = places_ref.shape[0] - 3
    width = values.shape[1] // count
    if width % 128:
        target[rows, :] = values
        return
    for block in range(count):
        to = pl.ds(pl.multiple_of(places_ref[block] * width, 128), width)
        target[rows, to] = values[:, block * width : (block + 1) * width]


def finish(middle, entering, attended, low, other_low, bias, places):
    rows, model = middle.shape

    def kernel(
        places_ref, middle_ref, entering_ref, attended_ref, low_ref, other_ref, bias_ref,
        output, stats
    ):
        branch = low_ref[...].astype(F32) + other_ref[...].astype(F32) + bias_ref[...]
        result = middle_ref[...] + branch
        place_blocks(output, slice(None), result.astype(BF16), places_ref)
        good = valid_rows(rows, places_ref)
        lane = lax.broadcasted_iota(jnp.int32, (1, 128), 1)
        row = jnp.where(lane == 5, column_sum(good), 0.0)
        terms = (entering_ref[...], attended_ref[...], middle_ref[...], branch, result)
        for index, term in enumerate(terms):
            total = jnp.sum(column_sum(term * term * good), axis=1, keepdims=True)
            row = jnp.where(lane == index, total, row)
        stats[...] = row

    in_vmem = pl.BlockSpec(memory_space=pltpu.VMEM)
    return pl.pallas_call(
        kernel,
        name="finish",
        in_specs=[pl.BlockSpec(memory_space=pltpu.SMEM)] + [in_vmem] * 6,
        out_specs=[in_vmem] * 2,
        out_shape=[shape_of(rows, model, BF16), shape_of(1, 128, F32)],
        cost_estimate=low_cost(),
    )(places, middle, entering, attended, low, other_low, bias)


def first_norm_back(
    inputs, gain, low, other_low, grad_middle, sums, up_sum, qv_sum, stats, places
):
    rows, model = inputs.shape

    def kernel(
        places_ref, inputs_ref, gain_ref, low_ref, other_ref, middle_ref,
        sums_ref, up_ref, qv_ref, stats_ref, grad_inputs, message
    ):
        grad = low_ref[...].astype(F32) + other_ref[...].astype(F32)
        valid = valid_rows(rows, places_ref)
        n, scale = norm_of(inputs_ref[...].astype(F32) * valid)
        total = middle_ref[...] + norm_grad(n, scale, gain_ref[...], grad)
        total = total * valid
        vectors = jnp.concatenate(
            [column_sum(grad * n), column_sum(grad), sums_ref[...]], axis=0
        )
        message[6:7, :] = up_ref[...]
        message[7:8, :] = jnp.zeros((1, model), F32)
        message[7:8, : qv_ref.shape[1]] = qv_ref[...]
        message[7:8, model - 128 :] = stats_ref[...]
        place_blocks(grad_inputs, slice(None), total, places_ref)
        place_blocks(message, slice(0, 6), vectors, places_ref)

    in_vmem = pl.BlockSpec(memory_space=pltpu.VMEM)
    return pl.pallas_call(
        kernel,
        name="first_norm_back",
        in_specs=[pl.BlockSpec(memory_space=pltpu.SMEM)] + [in_vmem] * 9,
        out_specs=[in_vmem] * 2,
        out_shape=[shape_of(rows, model, F32), shape_of(8, model, F32)],
        cost_estimate=low_cost(),
    )(
        places, inputs, gain, low, other_low, grad_middle, sums, up_sum, qv_sum, stats
    )


def halves_low(own, other):
    low = round_low(own + swap(other, "ctx").astype(F32))
    return low, swap(low, "tp")


def halves_sum(own, other):
    low = round_low(own + swap(other, "ctx").astype(F32))
    return low.astype(F32) + swap(low, "tp").astype(F32)


def coded(values):
    high = lax.reduce_precision(values, 8, 7)
    return rows_of(high.astype(BF16), round_low(values - high))


def decoded(rows):
    return lower(rows).astype(F32) + upper(rows).astype(F32)


def with_other(own):
    return jnp.concatenate([own, swap(own, "ctx")], axis=0)


def body(
    inputs,
    lengths,
    grad_out,
    ln1_gain,
    ln1_shift,
    w_qkv,
    b_qv,
    w_proj,
    b_proj,
    ln2_gain,
    ln2_shift,
    w_up,
    b_up,
    w_down,
    b_down,
):
    n = lax.axis_size("fsdp")
    cube = is_cube()
    core = lax.axis_index("ctx")
    place = lax.axis_index("fsdp")
    rows = w_up.shape[0]
    head_cols = w_proj.shape[1] // 2
    hidden = w_up.shape[1] // 2
    own_slots = inputs.shape[1]
    width = D // n

    qkv_halves = w_qkv.reshape(rows, 3, 2, head_cols)
    proj_halves = w_proj.reshape(rows, 2, head_cols)
    up_halves = w_up.reshape(rows, 2, hidden)
    down_halves = w_down.reshape(rows, 2, hidden)

    def first_half(which):
        return jnp.concatenate(
            [
                lax.dynamic_index_in_dim(qkv_halves, which, 2, keepdims=False).reshape(
                    rows, 3 * head_cols
                ),
                lax.dynamic_index_in_dim(proj_halves, which, 1, keepdims=False),
            ],
            axis=1,
        )

    def half_of(halves, which):
        return lax.dynamic_index_in_dim(halves, which, 1, keepdims=False)

    def by_core(own, other, axis):
        return jnp.where(
            core == 0,
            jnp.concatenate([own, other], axis=axis),
            jnp.concatenate([other, own], axis=axis),
        )

    small = jnp.concatenate(
        [
            jnp.stack([ln1_gain, ln1_shift, b_proj, ln2_gain, ln2_shift, b_down, b_qv[:, 0]]),
            b_up.reshape(2, rows),
        ]
    )
    small_both = by_core(small, swap(small, "ctx"), 1)
    first_own, first_other = first_half(core), first_half(1 - core)
    first_mine = by_core(first_own, swap(first_other, "ctx"), 0)
    small_flat = jnp.zeros((16 * 2 * rows,), BF16)
    small_flat = small_flat.at[: 9 * 2 * rows].set(small_both.reshape(-1))
    cols = first_mine.shape[1]
    small_rows = -(-16 * 2 * rows // cols)
    small_rows_padded = -(-small_rows // 8) * 8
    small_block = jnp.zeros((small_rows_padded * cols,), BF16)
    small_block = small_block.at[: 16 * 2 * rows].set(small_flat).reshape(small_rows_padded, cols)

    first_shard = jnp.concatenate([first_mine, small_block], axis=0)
    first_shard, inputs, grad_out, up_halves, down_halves = tie(
        first_shard, inputs, grad_out, up_halves, down_halves
    )
    u, d = (
        by_core(half_of(t, core), swap(half_of(t, 1 - core), "ctx"), 0)
        for t in (up_halves, down_halves)
    )
    absolute, relative = absolute_places(), relative_blocks()

    def to_relative(array):
        blocks = array.reshape(array.shape[0], n, width)
        return jnp.take(blocks, absolute, axis=1).reshape(array.shape)

    grad_own = to_relative(grad_out[0])
    length = lengths[0]
    own_ids = core * own_slots + jnp.arange(own_slots, dtype=jnp.int32)
    other_ids = (1 - core) * own_slots + jnp.arange(own_slots, dtype=jnp.int32)
    slot_ids = jnp.concatenate([own_ids, other_ids])
    key_valid = slot_ids < length
    row_valid = key_valid.astype(F32)[:, None]
    places = jnp.concatenate([absolute, jnp.stack([core, core * own_slots, length])])

    inputs_own = to_relative(inputs[0])
    entering_all = with_other(inputs_own).astype(F32) * row_valid
    grads = (grad_own, swap(grad_own, "ctx"))
    normal_one, _ = norm_of(entering_all)
    slots = 2 * own_slots
    f = first_shard
    if cube:
        f_far, f_x = flip(f, FAR_BIT), flip(f, X_BIT)
        grad_far = flip(grad_own[:, D // 2 :], X_BIT)
        f_far, f_x, grad_far, u, d = tie(f_far, f_x, grad_far, u, d)
        u_x = flip(u, X_BIT)
        f_near = flip(rows_of(f, f_far), NEAR_BIT)
        u_far, f_far_x, d_x = flip(u, FAR_BIT), flip(f_far, X_BIT), flip(d, X_BIT)
        f_near, u_far, f_far_x, u_x, d_x, u, d = tie(f_near, u_far, f_far_x, u_x, d_x, u, d)
        u_near = flip(rows_of(u, u_far), NEAR_BIT)
        d_far, f_near_x, u_far_x = flip(d, FAR_BIT), flip(f_near, X_BIT), flip(u_far, X_BIT)
        d_far, f_near_x, u_far_x, u_near, d, normal_one = tie(
            d_far, f_near_x, u_far_x, u_near, d, normal_one
        )
        d_near = flip(rows_of(d, d_far), NEAR_BIT)
        u_near_x = flip(u_near, X_BIT)
        first_pieces = [f, f_far, f_near, f_x, f_far_x, f_near_x]
    else:
        first_pieces, up_pieces, down_pieces = (
            [lax.all_gather(t, "fsdp", tiled=True)] for t in (f, u, d)
        )
    block, pitch = 2 * rows, 2 * rows + small_rows_padded
    vectors = qv_bias = None
    if not cube:
        whole = first_pieces[0].reshape(n, pitch, cols)
        first_pieces, pitch = [whole[:, :block].reshape(D, cols)], block
        small_abs = whole[:, block:].reshape(n, -1)[:, : 16 * 2 * rows]
        small_abs = small_abs.reshape(n, 16, 2 * rows).astype(F32)
        vectors = small_abs.transpose(1, 0, 2).reshape(16, D)
        qv_all = small_abs[:, 6].reshape(2, 2, head_cols)
        qv_bias = lax.dynamic_index_in_dim(qv_all, core, 1, keepdims=False)

    key_mask = row_valid.reshape(1, slots)
    query, key, value, context, att_own, att_other, normed, *found = attention(
        normal_one, vectors, qv_bias, key_mask, first_pieces, block, pitch, places
    )
    if cube:
        vectors, vectors_abs = found
        small_abs = vectors_abs.reshape(16, n, 2 * rows).transpose(1, 0, 2)
    gain_one, _, proj_bias, gain_two, shift_two, down_bias = (vectors[i] for i in range(6))
    up_all = small_abs[:, 7:9].reshape(n, 2, 2, rows).transpose(0, 2, 1, 3).reshape(2, hidden)
    up_bias = lax.dynamic_index_in_dim(up_all, core, 0, keepdims=False)
    if cube:
        d_near, u_near_x, d_far, att_own, att_other = tie(
            d_near, u_near_x, d_far, att_own, att_other
        )
        d_rest = rows_of(d_far, d_near)
        up_pieces = [u, u_far, u_near, u_x, u_far_x, u_near_x]
    att_low = round_low(att_own + swap(att_other, "ctx").astype(F32))
    if cube:
        att_low, d_rest = tie(att_low, d_rest)
        d_rest_x = flip(d_rest, X_BIT)
    att_tp = swap(att_low, "tp")
    attended = att_low.astype(F32) + att_tp.astype(F32) + proj_bias
    entering = entering_all[:own_slots]
    middle = entering + attended
    normal_two, _ = norm_of(middle)
    normed_two_own = (normal_two * gain_two + shift_two).astype(BF16)
    normed_two_other = swap(normed_two_own, "ctx")
    active, slope = hidden_layer(
        normed_two_own, normed_two_other, normed, up_bias[None], up_pieces, block
    )
    if cube:
        active, slope, d_rest_x = tie(active, slope, d_rest_x)
        active_far = flip(active, X_BIT)
        down_pieces = [d, d_far, d_near, d_x, d_rest_x]
    grad_pre, gn_own, gn_other, sum_up_bias = hidden_back(
        grads, slope, up_pieces, down_pieces, block
    )
    gn_low = round_low(gn_own + swap(gn_other, "ctx").astype(F32))
    if cube:
        gn_low, active = tie(gn_low, active)
    gn_tp = swap(gn_low, "tp")
    branch_own, branch_other = project_back(active, slots, down_pieces, block)
    if cube:
        gn_low, gn_tp, active_far, grad_pre, branch_own, branch_other = tie(
            gn_low, gn_tp, active_far, grad_pre, branch_own, branch_other
        )
        pre_far = flip(grad_pre, X_BIT)
        size, half = own_slots, D // 2
    grad_middle, grad_att_own, sums = second_norm_back(
        middle, gain_two[None], gn_low, gn_tp, grad_own
    )
    if cube:
        grad_att_own, active_far, branch_own, branch_other = tie(
            grad_att_own, active_far, branch_own, branch_other
        )
        att_far = flip(grad_att_own[:, half:], X_BIT)
        down_high, down_two = weight_grad(
            [
                (
                    [(t, 0, size, 0) for t in (*grads, grad_far, swap(grad_far, "ctx"))],
                    0,
                    hidden,
                )
            ],
            [(active, 0, slots), (active_far, 0, slots)],
            1,
        )
    grad_att_other = swap(grad_att_own, "ctx")
    if cube:
        down_high, grad_att_other = tie(down_high, grad_att_other)
        down_near = flip(down_high, NEAR_BIT)
    branch_low, branch_tp = halves_low(branch_own, branch_other)
    packed, gn_one_own, gn_one_other, sum_qv_bias = attention_back(
        (grad_att_own, grad_att_other), context, key_mask, query, key, value, first_pieces, block, pitch
    )
    if cube:
        pre_far, att_far, down_near, packed, gn_one_own, gn_one_other, branch_low, branch_tp = tie(
            pre_far, att_far, down_near, packed, gn_one_own, gn_one_other, branch_low, branch_tp
        )
        packed_far = flip(packed, X_BIT)
        down_far = flip(round_low(upper(down_two) + upper(down_near).astype(F32)), FAR_BIT)
        normed_swapped = swap(active_far[slots:], "ctx")
        up_high, up_two = weight_grad(
            [
                (
                    [
                        (normed_two_own, 0, size, 0),
                        (normed_two_other, 0, size, 0),
                        (active_far, slots, size, half),
                        (normed_swapped, 0, size, half),
                    ],
                    0,
                    hidden,
                )
            ],
            [(grad_pre, 0, slots), (pre_far, 0, slots)],
            1,
        )
    gn_one_low = round_low(gn_one_own + swap(gn_one_other, "ctx").astype(F32))
    if cube:
        gn_one_low, down_far = tie(gn_one_low, down_far)
    gn_one_tp = swap(gn_one_low, "tp")
    if cube:
        att_swapped = swap(att_far, "ctx")
        up_near = flip(up_high, NEAR_BIT)
        *first_high, first_two = weight_grad(
            [
                (
                    [
                        (normed, 0, slots, 0),
                        (active_far, slots, size, 0),
                        (normed_swapped, 0, size, 0),
                    ],
                    0,
                    3 * head_cols,
                ),
                (
                    [
                        (t, 0, size, 0)
                        for t in (grad_att_own, grad_att_other, att_far, att_swapped)
                    ],
                    3 * head_cols,
                    4 * head_cols,
                ),
            ],
            [(packed, 0, slots), (packed_far, 0, slots)],
            2,
        )
        first_high, gn_one_low, gn_one_tp, up_near = tie(
            first_high, gn_one_low, gn_one_tp, up_near
        )
        up_far = flip(round_low(upper(up_two) + upper(up_near).astype(F32)), FAR_BIT)
    else:
        sum_down = scatter_sum(contract(rows_of(*grads), active[:slots], 0, 0))
        sum_up = scatter_sum(contract(rows_of(normed_two_own, normed_two_other), grad_pre, 0, 0))
        sum_first = jnp.concatenate(
            [
                scatter_sum(contract(normed, packed[:, : 3 * head_cols], 0, 0)),
                scatter_sum(
                    contract(rows_of(grad_att_own, grad_att_other), context, 0, 0)
                ),
            ],
            axis=1,
        )
    output, stats = finish(
        middle, entering, attended, branch_low, branch_tp, down_bias[None], places
    )
    output = output[None]
    grad_inputs, message = first_norm_back(
        inputs_own,
        gain_one[None],
        gn_one_low,
        gn_one_tp,
        grad_middle,
        sums,
        sum_up_bias,
        sum_qv_bias,
        stats,
        places,
    )
    grad_inputs = grad_inputs[None]

    if cube:
        message = message + flip(message, X_BIT)
        first_near = [flip(rows_of(first_high[1], coded(message)), NEAR_BIT)]
        first_near[0], first_high, up_far = tie(first_near[0], first_high, up_far)
        message = message + decoded(first_near[0][block:])
        first_low = round_low(upper(first_two) + first_near[0][:block].astype(F32))
        far_rows, first_rest = tie(rows_of(first_low, coded(message)), first_high[0])
        first_far = flip(far_rows, FAR_BIT)
        first_near.append(flip(first_rest, NEAR_BIT))
        first_near[1], up_far = tie(first_near[1], up_far)
        sum_first = (
            lower(first_two) + first_near[1].astype(F32) + first_far[:block].astype(F32)
        )
        sum_down = lower(down_two) + lower(down_near).astype(F32) + down_far.astype(F32)
        sum_up = lower(up_two) + lower(up_near).astype(F32) + up_far.astype(F32)
        message = message + decoded(first_far[block:])
    else:
        message = lax.psum(message, "fsdp")
    other_message = swap(message, "ctx")
    at = 2 * place + core
    vector_own = lax.dynamic_slice_in_dim(
        message[:6] + other_message[:6], at * rows, rows, 1
    )
    totals = (message[7] + other_message[7])[D - 128 : D - 122]
    rms = jnp.sqrt(totals[:5] / (totals[5] * D))
    qv_sum = by_core(
        message[7, : 2 * head_cols].reshape(2, 1, head_cols),
        other_message[7, : 2 * head_cols].reshape(2, 1, head_cols),
        1,
    ).reshape(-1)
    qv_mine = lax.dynamic_slice_in_dim(qv_sum, at * rows, rows, 0)
    up_sum = by_core(message[6], other_message[6], 0)
    up_mine = lax.dynamic_slice_in_dim(up_sum, at * 2 * rows, 2 * rows, 0)

    def owned(total):
        mine = lax.dynamic_slice_in_dim(total, core * rows, rows, 0)
        theirs = swap(lax.dynamic_slice_in_dim(total, (1 - core) * rows, rows, 0), "ctx")
        return mine, theirs

    mine, theirs = owned(sum_first)
    parts = [
        by_core(mine[:, at : at + head_cols], theirs[:, at : at + head_cols], 1)
        for at in range(0, 4 * head_cols, head_cols)
    ]
    grad_w_qkv, grad_w_proj = jnp.stack(parts[:3], axis=1), parts[3]
    grad_w_up = by_core(*owned(sum_up), 1)
    grad_w_down = by_core(*owned(sum_down), 1)
    return (
        output,
        grad_inputs,
        vector_own[0],
        vector_own[1],
        grad_w_qkv,
        qv_mine[:, None],
        grad_w_proj,
        vector_own[2],
        vector_own[3],
        vector_own[4],
        grad_w_up,
        up_mine[:, None],
        grad_w_down,
        vector_own[5],
        rms,
    )


def solution(mesh):
    both = ("fsdp", "ctx")
    rows, vector, matrix = P("fsdp", "ctx", None), P(both), P(both, "tp")
    in_specs = (
        rows,
        P("fsdp"),
        rows,
        vector,
        vector,
        P(both, None, "tp"),
        matrix,
        matrix,
        vector,
        vector,
        vector,
        matrix,
        matrix,
        matrix,
        vector,
    )
    out_specs = (
        rows,
        rows,
        vector,
        vector,
        P(both, None, "tp"),
        matrix,
        matrix,
        vector,
        vector,
        vector,
        matrix,
        matrix,
        matrix,
        vector,
        P(),
    )
    return jax.shard_map(body, mesh=mesh, in_specs=in_specs, out_specs=out_specs, check_vma=False)
```

```python
import jax
import jax.numpy as jnp
from jax import lax
from jax.experimental import pallas as pl
from jax.experimental.pallas import tpu as pltpu
from jax.sharding import PartitionSpec as P

D = 1024
HD = 64
EPSILON = 1e-06
MASK_FILL = -1e30
ROOT_HALF = 0.7071067811865476
INV_ROOT_TWO_PI = 0.3989422804014327
F32 = jnp.float32
BF16 = jnp.bfloat16


def contract(left, right, left_dim, right_dim):
    return lax.dot_general(
        left, right, (((left_dim,), (right_dim,)), ((), ())), preferred_element_type=F32
    )


def round_low(values):
    return lax.reduce_precision(values, 8, 7).astype(BF16)


def swap(array, axis):
    return lax.ppermute(array, axis, [(0, 1), (1, 0)])


def flip(array, bit):
    n = lax.axis_size("fsdp")
    return lax.ppermute(array, "fsdp", [(i, i ^ bit) for i in range(n)])


X_BIT, NEAR_BIT, FAR_BIT = 1, 2, 4


def is_cube():
    return lax.axis_size("fsdp") == 8


def turned_bits(blocks):
    return (blocks % 2) * 4 + (blocks // 2 % 2) * 2 + blocks // 4


def relative_blocks():
    spots = jnp.arange(lax.axis_size("fsdp"), dtype=jnp.int32)
    if not is_cube():
        return spots
    return turned_bits(spots ^ lax.axis_index("fsdp"))


def absolute_places():
    blocks = jnp.arange(lax.axis_size("fsdp"), dtype=jnp.int32)
    if not is_cube():
        return blocks
    return turned_bits(blocks) ^ lax.axis_index("fsdp")


def tie(*values):
    return lax.optimization_barrier(values)


def rows_of(*pieces):
    return jnp.concatenate(pieces, axis=0)


def upper(array):
    return array[array.shape[0] // 2 :]


def lower(array):
    return array[: array.shape[0] // 2]


def scatter_sum(partial):
    low = round_low(partial)
    return lax.psum_scatter(low, "fsdp", scatter_dimension=0, tiled=True).astype(F32)


def low_cost():
    return pl.CostEstimate(flops=1000, transcendentals=0, bytes_accessed=1000)


def probabilities(query, key, mask):
    scores = contract(query, key, 1, 1) * (HD ** (-0.5))
    scores = jnp.where(mask > 0, scores, MASK_FILL)
    raised = jnp.exp(scores - jnp.max(scores, axis=-1, keepdims=True))
    return raised / jnp.sum(raised, axis=-1, keepdims=True)


def spans_of(pieces, block, pitch):
    spans, row = [], 0
    for index, piece in enumerate(pieces):
        for start in range(0, piece.shape[0], pitch):
            spans.append((index, start, row))
            row += block
    return spans


def merged(spans, block, pitch):
    if block != pitch:
        return [(index, start, row, block) for index, start, row in spans]
    joined = []
    for index, start, row in spans:
        if joined and joined[-1][0] == index:
            last = joined[-1]
            joined[-1] = (index, last[1], last[2], last[3] + block)
        else:
            joined.append((index, start, row, block))
    return joined


def times_pieces(left, pieces, spans, columns):
    total = None
    for index, start, row, size in spans:
        part = jnp.dot(
            left[:, row : row + size],
            pieces[index][start : start + size, columns],
            preferred_element_type=F32,
        )
        total = part if total is None else total + part
    return total


def times_pieces_back(left, pieces, spans, columns, own, other):
    half = own.shape[0]
    for index, start, row, size in spans:
        weight = pieces[index][start : start + size, columns]
        own[:, row : row + size] = contract(left[:half, :], weight, 1, 1)
        other[:, row : row + size] = contract(left[half:, :], weight, 1, 1).astype(BF16)


def shape_of(rows, columns, dtype):
    return jax.ShapeDtypeStruct((rows, columns), dtype)


def stacked(refs):
    return jnp.concatenate([ref[...] for ref in refs], axis=0)


def read_small(blocks, block, width, places_ref, relative, absolute):
    for index, (ref, start) in enumerate(blocks):
        lines = [
            ref[
                start + block + vector // 8 : start + block + vector // 8 + 1,
                vector % 8 * width : (vector % 8 + 1) * width,
            ]
            for vector in range(16)
        ]
        values = jnp.concatenate(lines, axis=0).astype(F32)
        relative[:, index * width : (index + 1) * width] = values
        to = pl.ds(pl.multiple_of(places_ref[index] * width, 128), width)
        absolute[:, to] = values


def attention(normal, vectors, bias, mask, pieces, block, pitch, places):
    slots, model = normal.shape
    width = pieces[0].shape[1] // 4
    half = slots // 2
    all_spans = spans_of(pieces, block, pitch)
    spans = merged(all_spans, block, pitch)
    given = [] if vectors is None else [vectors, bias]

    def kernel(places_ref, normal_ref, mask_ref, *refs):
        weights = refs[: len(pieces)]
        query, key, value, context, own, other, normed = refs[len(pieces) + len(given) :][:7]
        if given:
            small, own_bias = refs[len(pieces) : len(pieces) + 2]
            query_bias, value_bias = own_bias[0:1, :], own_bias[1:2, :]
        else:
            small, absolute = refs[-2:]
            blocks = [(weights[index], start) for index, start, _ in all_spans]
            read_small(blocks, block, model // len(blocks), places_ref, small, absolute)
            at = pl.multiple_of(places_ref[len(blocks)] * width, 128)
            query_bias = absolute[6:7, pl.ds(at, width)]
            value_bias = absolute[6:7, pl.ds(at + 2 * width, width)]
        normed[...] = (normal_ref[...] * small[0:1, :] + small[1:2, :]).astype(BF16)
        packed = times_pieces(normed, weights, spans, slice(0, 3 * width))
        query[...] = (packed[:, :width] + query_bias).astype(BF16)
        key[...] = packed[:, width : 2 * width].astype(BF16)
        value[...] = (packed[:, 2 * width :] + value_bias).astype(BF16)
        valid = mask_ref[...]
        parts = []
        for head in range(width // HD):
            at = slice(head * HD, (head + 1) * HD)
            prob = probabilities(query[:, at], key[:, at], valid)
            parts.append(jnp.dot(prob.astype(BF16), value[:, at], preferred_element_type=F32))
        context[...] = jnp.concatenate(parts, axis=1).astype(BF16)
        times_pieces_back(context, weights, spans, slice(3 * width, 4 * width), own, other)

    in_vmem = pl.BlockSpec(memory_space=pltpu.VMEM)
    small_shape = [] if given else [shape_of(16, model, F32)] * 2
    out_shape = (
        [shape_of(slots, width, BF16)] * 4
        + [shape_of(half, model, F32), shape_of(half, model, BF16), shape_of(slots, model, BF16)]
        + small_shape
    )
    return pl.pallas_call(
        kernel,
        name="attention",
        in_specs=[pl.BlockSpec(memory_space=pltpu.SMEM)]
        + [in_vmem] * (2 + len(pieces) + len(given)),
        out_specs=[in_vmem] * len(out_shape),
        out_shape=out_shape,
        cost_estimate=low_cost(),
    )(places, normal, mask, *pieces, *given)


def attention_back(grad_att, context, mask, query, key, value, pieces, block, pitch):
    slots, width = context.shape
    model = grad_att[0].shape[1]
    half = slots // 2
    scale = HD ** (-0.5)
    spans = merged(spans_of(pieces, block, pitch), block, pitch)

    def kernel(grad_own, grad_other, context_ref, mask_ref, query_ref, key_ref, value_ref, *refs):
        weights = refs[: len(pieces)]
        packed, own, other, bias_sum = refs[len(pieces) :]
        grad_ref = stacked((grad_own, grad_other))
        valid = mask_ref[...]
        grad_context = times_pieces(
            grad_ref, weights, spans, slice(3 * width, 4 * width)
        ).astype(BF16)
        queries, keys, values = [], [], []
        for head in range(width // HD):
            at = slice(head * HD, (head + 1) * HD)
            q, k, v, g = query_ref[:, at], key_ref[:, at], value_ref[:, at], grad_context[:, at]
            prob = probabilities(q, k, valid)
            grad_prob = contract(g, v, 1, 1)
            dots = jnp.sum(prob * grad_prob, axis=-1, keepdims=True)
            grad_scores = (prob * (grad_prob - dots)).astype(BF16)
            queries.append(jnp.dot(grad_scores, k, preferred_element_type=F32) * scale)
            keys.append(contract(grad_scores, q, 0, 0) * scale)
            values.append(contract(prob.astype(BF16), g, 0, 0))
        for kind, parts in enumerate((queries, keys, values)):
            joined = jnp.concatenate(parts, axis=1).astype(BF16)
            packed[:, kind * width : (kind + 1) * width] = joined
            if kind != 1:
                at = (kind // 2) * width
                bias_sum[:, at : at + width] = jnp.sum(joined.astype(F32), axis=0, keepdims=True)
        packed[:, 3 * width :] = context_ref[...]
        grads = packed.at[:, : 3 * width]
        times_pieces_back(grads, weights, spans, slice(0, 3 * width), own, other)

    return pl.pallas_call(
        kernel,
        name="attention_back",
        out_shape=[
            shape_of(slots, 4 * width, BF16),
            shape_of(half, model, F32),
            shape_of(half, model, BF16),
            shape_of(1, 2 * width, F32),
        ],
        cost_estimate=low_cost(),
    )(*grad_att, context, mask, query, key, value, *pieces)


def hidden_layer(own, other, normed, bias, pieces, block):
    half, model = own.shape
    slots, hidden = 2 * half, bias.shape[1]
    spans = merged(spans_of(pieces, block, block), block, block)

    def kernel(own_ref, other_ref, normed_ref, bias_ref, *refs):
        message, slope = refs[len(pieces) :]
        left = stacked((own_ref, other_ref))
        pre_act = times_pieces(left, refs[: len(pieces)], spans, slice(0, hidden))
        pre_act = pre_act + bias_ref[...]
        cumulative = 0.5 * (1.0 + lax.erf(pre_act * ROOT_HALF))
        message[:slots, :] = (pre_act * cumulative).astype(BF16)
        message[slots:, : model // 2] = normed_ref[:half, model // 2 :]
        message[slots:, model // 2 :] = own_ref[:, model // 2 :]
        slope[...] = cumulative + pre_act * (
            INV_ROOT_TWO_PI * jnp.exp(-0.5 * pre_act * pre_act)
        )

    return pl.pallas_call(
        kernel,
        name="hidden_layer",
        out_shape=[shape_of(slots + half, hidden, BF16), shape_of(slots, hidden, F32)],
        cost_estimate=low_cost(),
    )(own, other, normed, bias, *pieces)


def hidden_back(grads, slope, up_pieces, down_pieces, block):
    model = grads[0].shape[1]
    slots, hidden = slope.shape
    half = slots // 2
    spans = merged(spans_of(up_pieces, block, block), block, block)
    down_spans = merged(spans_of(down_pieces, block, block), block, block)
    count = len(up_pieces)
    total = count + len(down_pieces)

    def kernel(grad_own, grad_other, slope_ref, *refs):
        grad_ref = stacked((grad_own, grad_other))
        up, down = refs[:count], refs[count:total]
        grad_pre, own, other, bias_sum = refs[total:]
        grad_active = times_pieces(grad_ref, down, down_spans, slice(0, hidden))
        low = (grad_active * slope_ref[...]).astype(BF16)
        grad_pre[...] = low
        bias_sum[...] = jnp.sum(low.astype(F32), axis=0, keepdims=True)
        times_pieces_back(grad_pre, up, spans, slice(0, hidden), own, other)

    return pl.pallas_call(
        kernel,
        name="hidden_back",
        out_shape=[
            shape_of(slots, hidden, BF16),
            shape_of(half, model, F32),
            shape_of(half, model, BF16),
            shape_of(1, hidden, F32),
        ],
        cost_estimate=low_cost(),
    )(*grads, slope, *up_pieces, *down_pieces)


def project_back(values, slots, pieces, block):
    columns = values.shape[1]
    spans = merged(spans_of(pieces, block, block), block, block)
    half = slots // 2

    def kernel(values_ref, *refs):
        left = values_ref.at[:slots, :]
        times_pieces_back(left, refs[: len(pieces)], spans, slice(0, columns), refs[-2], refs[-1])

    return pl.pallas_call(
        kernel,
        name="project_back",
        out_shape=[shape_of(half, D, F32), shape_of(half, D, BF16)],
        cost_estimate=low_cost(),
    )(values, *pieces)


def weight_grad(groups, rights, parts):
    columns = rights[0][0].shape[1]
    cut = D // 4
    arrays, index_of = [], {}

    def index(array):
        if id(array) not in index_of:
            index_of[id(array)] = len(arrays)
            arrays.append(array)
        return index_of[id(array)]

    right_rows = [(index(array), row, count) for array, row, count in rights]
    left_rows = [
        ([(index(array), row, count, column) for array, row, count, column in lefts], lo, hi)
        for lefts, lo, hi in groups
    ]
    size = cut // parts

    def kernel(*refs):
        outs = refs[len(arrays) :]
        targets = [(outs[part], cut + part * size) for part in range(parts)] + [(outs[-1], 0)]
        for lefts, lo, hi in left_rows:
            right = jnp.concatenate(
                [refs[at][row : row + count, lo:hi] for at, row, count in right_rows], axis=0
            )
            for target, first in targets:
                left = jnp.concatenate(
                    [
                        refs[at][row : row + count, column + first : column + first + target.shape[0]]
                        for at, row, count, column in lefts
                    ],
                    axis=0,
                )
                target[:, lo:hi] = contract(left, right, 0, 0).astype(target.dtype)

    return pl.pallas_call(
        kernel,
        name="weight_grad",
        out_shape=[shape_of(size, columns, BF16)] * parts + [shape_of(cut, columns, F32)],
        cost_estimate=low_cost(),
    )(*arrays)


def norm_of(values):
    mean = jnp.mean(values, axis=-1, keepdims=True)
    centered = values - mean
    scale = lax.rsqrt(jnp.mean(centered * centered, axis=-1, keepdims=True) + EPSILON)
    return centered * scale, scale


def valid_rows(rows, places_ref):
    slot = lax.broadcasted_iota(jnp.int32, (rows, 1), 0) + places_ref[places_ref.shape[0] - 2]
    return (slot < places_ref[places_ref.shape[0] - 1]).astype(F32)


def norm_grad(normal, scale, gain, grad):
    weighted = grad * gain
    return scale * (
        weighted
        - jnp.mean(weighted, axis=-1, keepdims=True)
        - normal * jnp.mean(weighted * normal, axis=-1, keepdims=True)
    )


def column_sum(values):
    return jnp.sum(values, axis=0, keepdims=True)


def second_norm_back(middle, gain, low, other_low, grad_res):
    rows, model = middle.shape

    def kernel(middle_ref, gain_ref, low_ref, other_ref, res_ref, *outs):
        grad_middle, grad_att, sums = outs
        grad = low_ref[...].astype(F32) + other_ref[...].astype(F32)
        res = res_ref[...].astype(F32)
        n, scale = norm_of(middle_ref[...])
        total = res + norm_grad(n, scale, gain_ref[...], grad)
        grad_middle[...] = total
        rounded = total.astype(BF16)
        grad_att[...] = rounded
        sums[0:1, :] = column_sum(rounded.astype(F32))
        sums[1:2, :] = column_sum(grad * n)
        sums[2:3, :] = column_sum(grad)
        sums[3:4, :] = column_sum(res)

    return pl.pallas_call(
        kernel,
        name="second_norm_back",
        out_shape=[
            shape_of(rows, model, F32),
            shape_of(rows, model, BF16),
            shape_of(4, model, F32),
        ],
        cost_estimate=low_cost(),
    )(middle, gain, low, other_low, grad_res)


def place_blocks(target, rows, values, places_ref):
    count = places_ref.shape[0] - 3
    width = values.shape[1] // count
    if width % 128:
        target[rows, :] = values
        return
    for block in range(count):
        to = pl.ds(pl.multiple_of(places_ref[block] * width, 128), width)
        target[rows, to] = values[:, block * width : (block + 1) * width]


def finish(middle, entering, attended, low, other_low, bias, places):
    rows, model = middle.shape

    def kernel(
        places_ref, middle_ref, entering_ref, attended_ref, low_ref, other_ref, bias_ref,
        output, stats
    ):
        branch = low_ref[...].astype(F32) + other_ref[...].astype(F32) + bias_ref[...]
        result = middle_ref[...] + branch
        place_blocks(output, slice(None), result.astype(BF16), places_ref)
        good = valid_rows(rows, places_ref)
        lane = lax.broadcasted_iota(jnp.int32, (1, 128), 1)
        row = jnp.where(lane == 5, column_sum(good), 0.0)
        terms = (entering_ref[...], attended_ref[...], middle_ref[...], branch, result)
        for index, term in enumerate(terms):
            total = jnp.sum(column_sum(term * term * good), axis=1, keepdims=True)
            row = jnp.where(lane == index, total, row)
        stats[...] = row

    in_vmem = pl.BlockSpec(memory_space=pltpu.VMEM)
    return pl.pallas_call(
        kernel,
        name="finish",
        in_specs=[pl.BlockSpec(memory_space=pltpu.SMEM)] + [in_vmem] * 6,
        out_specs=[in_vmem] * 2,
        out_shape=[shape_of(rows, model, BF16), shape_of(1, 128, F32)],
        cost_estimate=low_cost(),
    )(places, middle, entering, attended, low, other_low, bias)


def first_norm_back(
    inputs, gain, low, other_low, grad_middle, sums, up_sum, qv_sum, stats, places
):
    rows, model = inputs.shape

    def kernel(
        places_ref, inputs_ref, gain_ref, low_ref, other_ref, middle_ref,
        sums_ref, up_ref, qv_ref, stats_ref, grad_inputs, message
    ):
        grad = low_ref[...].astype(F32) + other_ref[...].astype(F32)
        valid = valid_rows(rows, places_ref)
        n, scale = norm_of(inputs_ref[...].astype(F32) * valid)
        total = middle_ref[...] + norm_grad(n, scale, gain_ref[...], grad)
        total = total * valid
        vectors = jnp.concatenate(
            [column_sum(grad * n), column_sum(grad), sums_ref[...]], axis=0
        )
        message[6:7, :] = up_ref[...]
        message[7:8, :] = jnp.zeros((1, model), F32)
        message[7:8, : qv_ref.shape[1]] = qv_ref[...]
        message[7:8, model - 128 :] = stats_ref[...]
        place_blocks(grad_inputs, slice(None), total, places_ref)
        place_blocks(message, slice(0, 6), vectors, places_ref)

    in_vmem = pl.BlockSpec(memory_space=pltpu.VMEM)
    return pl.pallas_call(
        kernel,
        name="first_norm_back",
        in_specs=[pl.BlockSpec(memory_space=pltpu.SMEM)] + [in_vmem] * 9,
        out_specs=[in_vmem] * 2,
        out_shape=[shape_of(rows, model, F32), shape_of(8, model, F32)],
        cost_estimate=low_cost(),
    )(
        places, inputs, gain, low, other_low, grad_middle, sums, up_sum, qv_sum, stats
    )


def halves_low(own, other):
    low = round_low(own + swap(other, "ctx").astype(F32))
    return low, swap(low, "tp")


def halves_sum(own, other):
    low = round_low(own + swap(other, "ctx").astype(F32))
    return low.astype(F32) + swap(low, "tp").astype(F32)


def coded(values):
    high = lax.reduce_precision(values, 8, 7)
    return rows_of(high.astype(BF16), round_low(values - high))


def decoded(rows):
    return lower(rows).astype(F32) + upper(rows).astype(F32)


def with_other(own):
    return jnp.concatenate([own, swap(own, "ctx")], axis=0)


def body(
    inputs,
    lengths,
    grad_out,
    ln1_gain,
    ln1_shift,
    w_qkv,
    b_qv,
    w_proj,
    b_proj,
    ln2_gain,
    ln2_shift,
    w_up,
    b_up,
    w_down,
    b_down,
):
    n = lax.axis_size("fsdp")
    cube = is_cube()
    core = lax.axis_index("ctx")
    place = lax.axis_index("fsdp")
    rows = w_up.shape[0]
    head_cols = w_proj.shape[1] // 2
    hidden = w_up.shape[1] // 2
    own_slots = inputs.shape[1]
    width = D // n

    qkv_halves = w_qkv.reshape(rows, 3, 2, head_cols)
    proj_halves = w_proj.reshape(rows, 2, head_cols)
    up_halves = w_up.reshape(rows, 2, hidden)
    down_halves = w_down.reshape(rows, 2, hidden)

    def first_half(which):
        return jnp.concatenate(
            [
                lax.dynamic_index_in_dim(qkv_halves, which, 2, keepdims=False).reshape(
                    rows, 3 * head_cols
                ),
                lax.dynamic_index_in_dim(proj_halves, which, 1, keepdims=False),
            ],
            axis=1,
        )

    def half_of(halves, which):
        return lax.dynamic_index_in_dim(halves, which, 1, keepdims=False)

    def by_core(own, other, axis):
        return jnp.where(
            core == 0,
            jnp.concatenate([own, other], axis=axis),
            jnp.concatenate([other, own], axis=axis),
        )

    small = jnp.concatenate(
        [
            jnp.stack([ln1_gain, ln1_shift, b_proj, ln2_gain, ln2_shift, b_down, b_qv[:, 0]]),
            b_up.reshape(2, rows),
        ]
    )
    small_both = by_core(small, swap(small, "ctx"), 1)
    first_own, first_other = first_half(core), first_half(1 - core)
    first_mine = by_core(first_own, swap(first_other, "ctx"), 0)
    small_flat = jnp.zeros((16 * 2 * rows,), BF16)
    small_flat = small_flat.at[: 9 * 2 * rows].set(small_both.reshape(-1))
    cols = first_mine.shape[1]
    small_rows = -(-16 * 2 * rows // cols)
    small_rows_padded = -(-small_rows // 8) * 8
    small_block = jnp.zeros((small_rows_padded * cols,), BF16)
    small_block = small_block.at[: 16 * 2 * rows].set(small_flat).reshape(small_rows_padded, cols)

    first_shard = jnp.concatenate([first_mine, small_block], axis=0)
    first_shard, inputs, grad_out, up_halves, down_halves = tie(
        first_shard, inputs, grad_out, up_halves, down_halves
    )
    u, d = (
        by_core(half_of(t, core), swap(half_of(t, 1 - core), "ctx"), 0)
        for t in (up_halves, down_halves)
    )
    absolute, relative = absolute_places(), relative_blocks()

    def to_relative(array):
        blocks = array.reshape(array.shape[0], n, width)
        return jnp.take(blocks, absolute, axis=1).reshape(array.shape)

    grad_own = to_relative(grad_out[0])
    length = lengths[0]
    own_ids = core * own_slots + jnp.arange(own_slots, dtype=jnp.int32)
    other_ids = (1 - core) * own_slots + jnp.arange(own_slots, dtype=jnp.int32)
    slot_ids = jnp.concatenate([own_ids, other_ids])
    key_valid = slot_ids < length
    row_valid = key_valid.astype(F32)[:, None]
    places = jnp.concatenate([absolute, jnp.stack([core, core * own_slots, length])])

    inputs_own = to_relative(inputs[0])
    entering_all = with_other(inputs_own).astype(F32) * row_valid
    grads = (grad_own, swap(grad_own, "ctx"))
    normal_one, _ = norm_of(entering_all)
    entering = entering_all[:own_slots]
    slots = 2 * own_slots
    f = first_shard
    if cube:
        f_far, f_x = flip(f, FAR_BIT), flip(f, X_BIT)
        grad_far = flip(grad_own[:, D // 2 :], X_BIT)
        f_far, f_x, grad_far, u, d = tie(f_far, f_x, grad_far, u, d)
        u_x = flip(u, X_BIT)
        f_near = flip(rows_of(f, f_far), NEAR_BIT)
        u_far, f_far_x, d_x = flip(u, FAR_BIT), flip(f_far, X_BIT), flip(d, X_BIT)
        f_near, u_far, f_far_x, u_x, d_x, u, d = tie(f_near, u_far, f_far_x, u_x, d_x, u, d)
        u_near = flip(rows_of(u, u_far), NEAR_BIT)
        d_far, f_near_x, u_far_x = flip(d, FAR_BIT), flip(f_near, X_BIT), flip(u_far, X_BIT)
        d_far, f_near_x, u_far_x, u_near, d, normal_one, entering = tie(
            d_far, f_near_x, u_far_x, u_near, d, normal_one, entering
        )
        d_near = flip(rows_of(d, d_far), NEAR_BIT)
        u_near_x = flip(u_near, X_BIT)
        first_pieces = [f, f_far, f_near, f_x, f_far_x, f_near_x]
    else:
        first_pieces, up_pieces, down_pieces = (
            [lax.all_gather(t, "fsdp", tiled=True)] for t in (f, u, d)
        )
    block, pitch = 2 * rows, 2 * rows + small_rows_padded
    vectors = qv_bias = None
    if not cube:
        whole = first_pieces[0].reshape(n, pitch, cols)
        first_pieces, pitch = [whole[:, :block].reshape(D, cols)], block
        small_abs = whole[:, block:].reshape(n, -1)[:, : 16 * 2 * rows]
        small_abs = small_abs.reshape(n, 16, 2 * rows).astype(F32)
        vectors = small_abs.transpose(1, 0, 2).reshape(16, D)
        qv_all = small_abs[:, 6].reshape(2, 2, head_cols)
        qv_bias = lax.dynamic_index_in_dim(qv_all, core, 1, keepdims=False)

    key_mask = row_valid.reshape(1, slots)
    query, key, value, context, att_own, att_other, normed, *found = attention(
        normal_one, vectors, qv_bias, key_mask, first_pieces, block, pitch, places
    )
    if cube:
        vectors, vectors_abs = found
        small_abs = vectors_abs.reshape(16, n, 2 * rows).transpose(1, 0, 2)
    gain_one, _, proj_bias, gain_two, shift_two, down_bias = (vectors[i] for i in range(6))
    up_all = small_abs[:, 7:9].reshape(n, 2, 2, rows).transpose(0, 2, 1, 3).reshape(2, hidden)
    up_bias = lax.dynamic_index_in_dim(up_all, core, 0, keepdims=False)
    if cube:
        d_near, u_near_x, d_far, att_own, att_other = tie(
            d_near, u_near_x, d_far, att_own, att_other
        )
        d_rest = rows_of(d_far, d_near)
        up_pieces = [u, u_far, u_near, u_x, u_far_x, u_near_x]
    att_low = round_low(att_own + swap(att_other, "ctx").astype(F32))
    if cube:
        att_low, d_rest = tie(att_low, d_rest)
        d_rest_x = flip(d_rest, X_BIT)
    att_tp = swap(att_low, "tp")
    attended = att_low.astype(F32) + att_tp.astype(F32) + proj_bias
    middle = entering + attended
    normal_two, _ = norm_of(middle)
    normed_two_own = (normal_two * gain_two + shift_two).astype(BF16)
    normed_two_other = swap(normed_two_own, "ctx")
    active, slope = hidden_layer(
        normed_two_own, normed_two_other, normed, up_bias[None], up_pieces, block
    )
    if cube:
        active, slope, d_rest_x = tie(active, slope, d_rest_x)
        active_far = flip(active, X_BIT)
        down_pieces = [d, d_far, d_near, d_x, d_rest_x]
    grad_pre, gn_own, gn_other, sum_up_bias = hidden_back(
        grads, slope, up_pieces, down_pieces, block
    )
    gn_low = round_low(gn_own + swap(gn_other, "ctx").astype(F32))
    if cube:
        gn_low, active = tie(gn_low, active)
    gn_tp = swap(gn_low, "tp")
    branch_own, branch_other = project_back(active, slots, down_pieces, block)
    if cube:
        gn_low, gn_tp, active_far, grad_pre, branch_own, branch_other = tie(
            gn_low, gn_tp, active_far, grad_pre, branch_own, branch_other
        )
        pre_far = flip(grad_pre, X_BIT)
        size, half = own_slots, D // 2
    grad_middle, grad_att_own, sums = second_norm_back(
        middle, gain_two[None], gn_low, gn_tp, grad_own
    )
    if cube:
        grad_att_own, active_far, branch_own, branch_other = tie(
            grad_att_own, active_far, branch_own, branch_other
        )
        att_far = flip(grad_att_own[:, half:], X_BIT)
        down_high, down_two = weight_grad(
            [
                (
                    [(t, 0, size, 0) for t in (*grads, grad_far, swap(grad_far, "ctx"))],
                    0,
                    hidden,
                )
            ],
            [(active, 0, slots), (active_far, 0, slots)],
            1,
        )
    grad_att_other = swap(grad_att_own, "ctx")
    if cube:
        down_high, grad_att_other = tie(down_high, grad_att_other)
        down_near = flip(down_high, NEAR_BIT)
    branch_low, branch_tp = halves_low(branch_own, branch_other)
    packed, gn_one_own, gn_one_other, sum_qv_bias = attention_back(
        (grad_att_own, grad_att_other), context, key_mask, query, key, value, first_pieces, block, pitch
    )
    if cube:
        pre_far, att_far, down_near, packed, gn_one_own, gn_one_other, branch_low, branch_tp = tie(
            pre_far, att_far, down_near, packed, gn_one_own, gn_one_other, branch_low, branch_tp
        )
        packed_far = flip(packed, X_BIT)
        down_far = flip(round_low(upper(down_two) + upper(down_near).astype(F32)), FAR_BIT)
        normed_swapped = swap(active_far[slots:], "ctx")
        up_high, up_two = weight_grad(
            [
                (
                    [
                        (normed_two_own, 0, size, 0),
                        (normed_two_other, 0, size, 0),
                        (active_far, slots, size, half),
                        (normed_swapped, 0, size, half),
                    ],
                    0,
                    hidden,
                )
            ],
            [(grad_pre, 0, slots), (pre_far, 0, slots)],
            1,
        )
    gn_one_low = round_low(gn_one_own + swap(gn_one_other, "ctx").astype(F32))
    if cube:
        gn_one_low, down_far = tie(gn_one_low, down_far)
    gn_one_tp = swap(gn_one_low, "tp")
    if cube:
        att_swapped = swap(att_far, "ctx")
        up_near = flip(up_high, NEAR_BIT)
        *first_high, first_two = weight_grad(
            [
                (
                    [
                        (normed, 0, slots, 0),
                        (active_far, slots, size, 0),
                        (normed_swapped, 0, size, 0),
                    ],
                    0,
                    3 * head_cols,
                ),
                (
                    [
                        (t, 0, size, 0)
                        for t in (grad_att_own, grad_att_other, att_far, att_swapped)
                    ],
                    3 * head_cols,
                    4 * head_cols,
                ),
            ],
            [(packed, 0, slots), (packed_far, 0, slots)],
            2,
        )
        first_high, gn_one_low, gn_one_tp, up_near = tie(
            first_high, gn_one_low, gn_one_tp, up_near
        )
        up_far = flip(round_low(upper(up_two) + upper(up_near).astype(F32)), FAR_BIT)
    else:
        sum_down = scatter_sum(contract(rows_of(*grads), active[:slots], 0, 0))
        sum_up = scatter_sum(contract(rows_of(normed_two_own, normed_two_other), grad_pre, 0, 0))
        sum_first = jnp.concatenate(
            [
                scatter_sum(contract(normed, packed[:, : 3 * head_cols], 0, 0)),
                scatter_sum(
                    contract(rows_of(grad_att_own, grad_att_other), context, 0, 0)
                ),
            ],
            axis=1,
        )
    output, stats = finish(
        middle, entering, attended, branch_low, branch_tp, down_bias[None], places
    )
    output = output[None]
    grad_inputs, message = first_norm_back(
        inputs_own,
        gain_one[None],
        gn_one_low,
        gn_one_tp,
        grad_middle,
        sums,
        sum_up_bias,
        sum_qv_bias,
        stats,
        places,
    )
    grad_inputs = grad_inputs[None]

    if cube:
        message = message + flip(message, X_BIT)
        first_near = [flip(rows_of(first_high[1], coded(message)), NEAR_BIT)]
        first_near[0], first_high, up_far = tie(first_near[0], first_high, up_far)
        message = message + decoded(first_near[0][block:])
        first_low = round_low(upper(first_two) + first_near[0][:block].astype(F32))
        far_rows, first_rest = tie(rows_of(first_low, coded(message)), first_high[0])
        first_far = flip(far_rows, FAR_BIT)
        first_near.append(flip(first_rest, NEAR_BIT))
        first_near[1], up_far = tie(first_near[1], up_far)
        sum_first = (
            lower(first_two) + first_near[1].astype(F32) + first_far[:block].astype(F32)
        )
        sum_down = lower(down_two) + lower(down_near).astype(F32) + down_far.astype(F32)
        sum_up = lower(up_two) + lower(up_near).astype(F32) + up_far.astype(F32)
        message = message + decoded(first_far[block:])
    else:
        message = lax.psum(message, "fsdp")
    other_message = swap(message, "ctx")
    at = 2 * place + core
    vector_own = lax.dynamic_slice_in_dim(
        message[:6] + other_message[:6], at * rows, rows, 1
    )
    totals = (message[7] + other_message[7])[D - 128 : D - 122]
    rms = jnp.sqrt(totals[:5] / (totals[5] * D))
    qv_sum = by_core(
        message[7, : 2 * head_cols].reshape(2, 1, head_cols),
        other_message[7, : 2 * head_cols].reshape(2, 1, head_cols),
        1,
    ).reshape(-1)
    qv_mine = lax.dynamic_slice_in_dim(qv_sum, at * rows, rows, 0)
    up_sum = by_core(message[6], other_message[6], 0)
    up_mine = lax.dynamic_slice_in_dim(up_sum, at * 2 * rows, 2 * rows, 0)

    def owned(total):
        mine = lax.dynamic_slice_in_dim(total, core * rows, rows, 0)
        theirs = swap(lax.dynamic_slice_in_dim(total, (1 - core) * rows, rows, 0), "ctx")
        return mine, theirs

    mine, theirs = owned(sum_first)
    parts = [
        by_core(mine[:, at : at + head_cols], theirs[:, at : at + head_cols], 1)
        for at in range(0, 4 * head_cols, head_cols)
    ]
    grad_w_qkv, grad_w_proj = jnp.stack(parts[:3], axis=1), parts[3]
    grad_w_up = by_core(*owned(sum_up), 1)
    grad_w_down = by_core(*owned(sum_down), 1)
    return (
        output,
        grad_inputs,
        vector_own[0],
        vector_own[1],
        grad_w_qkv,
        qv_mine[:, None],
        grad_w_proj,
        vector_own[2],
        vector_own[3],
        vector_own[4],
        grad_w_up,
        up_mine[:, None],
        grad_w_down,
        vector_own[5],
        rms,
    )


def solution(mesh):
    both = ("fsdp", "ctx")
    rows, vector, matrix = P("fsdp", "ctx", None), P(both), P(both, "tp")
    in_specs = (
        rows,
        P("fsdp"),
        rows,
        vector,
        vector,
        P(both, None, "tp"),
        matrix,
        matrix,
        vector,
        vector,
        vector,
        matrix,
        matrix,
        matrix,
        vector,
    )
    out_specs = (
        rows,
        rows,
        vector,
        vector,
        P(both, None, "tp"),
        matrix,
        matrix,
        vector,
        vector,
        vector,
        matrix,
        matrix,
        matrix,
        vector,
        P(),
    )
    return jax.shard_map(body, mesh=mesh, in_specs=in_specs, out_specs=out_specs, check_vma=False)
```
